128 devices in a mesh: section: 4 (over x), seq: 32 (over z, y, core).
Axes of the slice: x: 4, y: 4, z: 4, core: 2. Of those that a mesh axis runs over, the one named last changes fastest.
Arguments:
- frames_in: bfloat16 [4, 64, 128, 1024], P(None, 'seq'), may hold values from -6 to 6
- order: int32 [4], replicated, may hold values from 0 to 3, each once
- owner: int32 [128], replicated, may hold values from 0 to 31, as said below
- qkv_weight: bfloat16 [4, 1024, 3072], P('section'), may hold values from -1 to 1
- out_weight: bfloat16 [4, 1024, 1024], P('section'), may hold values from -0.1875 to 0.1875
- gains: float32 [4, 1024], P('section'), may hold values from 0.1 to 1.9
Outputs:
- layers_out: bfloat16 [4, 64, 256, 1024], P('section', None, 'seq')
The draws below stay inside these ranges and needn't reach their ends.
Inputs may be any that keep to these rules, and one draw needn't show every extreme that they name: `owner`: no device owns more than 8 rows, and some device owns exactly 8.
All inputs are finite; a program needn't handle non-finite values.
Results may differ from the reference program's by a relative error of at most 0.02.
Values may be sent and summed in bfloat16 or wider, within the bound.
A program may use at most 128 MiB of HBM per device.

```python
import jax
import jax.numpy as jnp
from jax import lax

D = 1024
HEADS = 16
HEAD_DIM = 64
IMG_ROWS = 128
FRAMES = 4
COLS = 16
LINES = 64
MAX_ROWS = 8
CLIPS = 4
LAYERS = 4
N_SEQ = 32


def draw_owner(key, part):
    per_device = IMG_ROWS // N_SEQ
    first_key, second_key = jax.random.split(jax.random.fold_in(key, 7))
    devices = jax.random.permutation(first_key, N_SEQ).astype(jnp.int32)
    pattern = jnp.array([2 * per_device, per_device + per_device // 2, per_device // 2, 0], dtype=jnp.int32)
    counts = pattern[jnp.arange(N_SEQ, dtype=jnp.int32) % 4]
    ends = jnp.cumsum(counts)
    position = jnp.arange(IMG_ROWS, dtype=jnp.int32)
    placed = jnp.sum((position[:, None] >= ends[None, :]).astype(jnp.int32), axis=1)
    sorted_owner = devices[placed]
    shuffle = jax.random.permutation(second_key, IMG_ROWS).astype(jnp.int32)
    owner = jnp.zeros((IMG_ROWS,), jnp.int32).at[shuffle].set(sorted_owner)
    return owner.astype(jnp.int32)


def draw_qkv_weight(key, part):
    base_key = jax.random.fold_in(jax.random.fold_in(key, 31), 0)
    spread = D ** (-0.5)
    matrix = jax.random.normal(base_key, (LAYERS, D, 3 * D), jnp.float32) * spread
    return jnp.clip(matrix, -1.0, 1.0).astype(jnp.bfloat16)


def block_scale(own_key, extent, shards, least, high):
    factor_of = 1.0
    for dim, parts in shards:
        heights = jax.random.uniform(jax.random.fold_in(jax.random.fold_in(own_key, 6), dim), (parts,), jnp.float32, least / len(shards), high / len(shards))
        factor_of = factor_of * jnp.repeat(jnp.exp(heights), extent[dim] // parts).reshape((-1,) + (1,) * (len(extent) - 1 - dim))
    return factor_of


def normal_values(rng, extent, scale, bound, shards=(), kind=jnp.bfloat16):
    values = scale * jax.random.normal(rng, extent, jnp.float32)
    if shards:
        values = values * block_scale(rng, extent, shards, -0.22, 0.18)
    return jnp.clip(values, -bound, bound).astype(kind)


def setup_inputs(seed: int = 0) -> dict:
    keys = jax.random.split(jax.random.key(seed), 7)
    return {
        "frames_in": normal_values(keys[0], (CLIPS, LINES, IMG_ROWS, D), 1.0, 6.0, ((1, 32),)),
        "order": jax.random.permutation(keys[1], CLIPS).astype(jnp.int32),
        "owner": draw_owner(jax.random.fold_in(keys[6], 71), 0),
        "qkv_weight": draw_qkv_weight(jax.random.fold_in(keys[6], 71), 0),
        "out_weight": normal_values(keys[4], (LAYERS, D, D), D ** -0.5, 0.1875, ((0, 4),)),
        "gains": jnp.clip(1.0 + 0.18 * jax.random.normal(keys[5], (LAYERS, D), jnp.float32), 0.1, 1.9),
    }


def scaled_norm(volume, gain_row):
    values = volume.astype(jnp.float32)
    mean_square = lax.optimization_barrier(jnp.mean(values * values, axis=-1, keepdims=True))
    return (values * lax.rsqrt(mean_square + 1e-06) * gain_row.astype(jnp.float32)).astype(jnp.bfloat16)

def attention_layer(volume, gain_row, qkv_mat, out_mat, causal):
    extent_a, length, extent_c, features = volume.shape
    normed = scaled_norm(volume, gain_row)
    packed = jnp.dot(normed.reshape(-1, features), qkv_mat, preferred_element_type=jnp.float32)
    packed = packed.astype(jnp.bfloat16).reshape(extent_a, length, extent_c, 3, HEADS, HEAD_DIM)
    queries = packed[:, :, :, 0].astype(jnp.float32)
    key_rows = packed[:, :, :, 1].astype(jnp.float32)
    values = packed[:, :, :, 2].astype(jnp.float32)
    scores = jnp.einsum('alchd,amchd->achlm', queries, key_rows) * HEAD_DIM ** (-0.5)
    if causal:
        allowed = jnp.arange(length)[:, None] >= jnp.arange(length)[None, :]
        scores = jnp.where(allowed, scores, -1e+30)
    weights = jax.nn.softmax(scores, axis=-1).astype(jnp.bfloat16)
    context = jnp.einsum('achlm,amchd->alchd', weights.astype(jnp.float32), values)
    context = context.astype(jnp.bfloat16).reshape(-1, features)
    update = jnp.dot(context, out_mat, preferred_element_type=jnp.float32).reshape(volume.shape)
    return (volume.astype(jnp.float32) + update).astype(jnp.bfloat16)

def reference(frames_in, order, owner, qkv_weight, out_weight, gains):
    position = jnp.arange(IMG_ROWS, dtype=jnp.int32)
    alike = (owner[:, None] == owner[None, :]) & (position[:, None] < position[None, :])
    slot_of = lax.optimization_barrier(jnp.sum(alike.astype(jnp.int32), axis=0))
    device_ids = jnp.arange(N_SEQ, dtype=jnp.int32)
    slot_ids = jnp.arange(MAX_ROWS, dtype=jnp.int32)
    match = (owner[None, None, :] == device_ids[:, None, None]) & (slot_of[None, None, :] == slot_ids[None, :, None])
    chosen = lax.optimization_barrier(jnp.sum(jnp.where(match, position[None, None, :], 0), axis=2)).reshape(-1).astype(jnp.int32)
    present = jnp.any(match, axis=2).reshape(-1)
    outputs = []
    for turn in range(CLIPS):
        clip_lines = lax.dynamic_index_in_dim(frames_in, order[turn], 0, keepdims=False)
        mixed = attention_layer(clip_lines[:, :, None, :], gains[0], qkv_weight[0], out_weight[0], False)[:, :, 0, :]
        mixed = attention_layer(mixed.reshape(1, FRAMES, COLS * IMG_ROWS, D), gains[1], qkv_weight[1], out_weight[1], False)
        mixed = mixed.reshape(LINES, IMG_ROWS, D)
        for layer in (2, 3):
            mixed = attention_layer(mixed.reshape(FRAMES, COLS, IMG_ROWS, D), gains[layer], qkv_weight[layer], out_weight[layer], True)
            mixed = mixed.reshape(LINES, IMG_ROWS, D)
        picked = jnp.take(mixed, chosen, axis=1)
        picked = jnp.where(present[None, :, None], picked, jnp.zeros((), jnp.bfloat16))
        outputs.append(picked)
    return jnp.stack(outputs[::-1])
```

```python
import functools

import jax
import jax.numpy as jnp
from jax import lax
from jax.experimental import pallas as pl
from jax.experimental.pallas import tpu as pltpu
from jax.sharding import PartitionSpec as P

MESH = pl.DeviceIdType.MESH
HEADS = 16
FRAMES = 4


class Gather:
    def __init__(self, wq_in, wo_in, wq, wo, sems, use_dd=True):
        self.wq_in, self.wo_in, self.wq, self.wo = wq_in, wo_in, wq, wo
        (self.xs, self.xr, self.p1s, self.p1r, self.p2s, self.p2r, self.ds, self.dr, self.own) = sems
        self.x = lax.axis_index("section")
        q = lax.axis_index("seq")
        self.c = lax.rem(q, 2)
        self.y = lax.rem(q // 2, 4)
        self.z = q // 8
        self.q = q
        self.use_dd = use_dd
        self.pending = []
    def dev(self, dx=0, dy=0, dz=0, dc=0):
        x = lax.rem(self.x + (dx + 4), 4)
        y = lax.rem(self.y + (dy + 4), 4)
        z = lax.rem(self.z + (dz + 4), 4)
        c = lax.rem(self.c + dc, 2)
        return (x, (z * 4 + y) * 2 + c)
    def neighbours(self):
        return [self.dev(dx=1), self.dev(dx=-1), self.dev(dy=1), self.dev(dy=-1), self.dev(dz=1), self.dev(dz=-1), self.dev(dc=1)]
    def barrier(self):
        b = pltpu.get_barrier_semaphore()
        ns = self.neighbours()
        for n in ns:
            pl.semaphore_signal(b, inc=1, device_id=n, device_id_type=MESH)
        pl.semaphore_wait(b, len(ns))
    def copy(self, src, dst, ss, rs, dev):
        return pltpu.make_async_remote_copy(src_ref=src, dst_ref=dst, send_sem=ss, recv_sem=rs, device_id=dev, device_id_type=MESH)
    def send(self, src, dst, ss, rs, dev):
        cp = self.copy(src, dst, ss, rs, dev)
        cp.start()
        self.pending.append(cp)
    def recv(self, dst, ss, rs):
        self.copy(dst, dst, ss, rs, self.dev(dc=1)).wait_recv()
    def rows(self, ab, i=0, blk=0):
        y, z = self.y, self.z
        if ab == 0:
            major, minor = lax.rem(z + (blk + 4), 4), lax.rem(y + (i + 4), 4)
        else:
            major, minor = lax.rem(y + (blk + 4), 4), lax.rem(z + (i + 4), 4)
        return self.c * 512 + ab * 256 + major * 64, minor * 16
    def sl(self, l, ab, i):
        a, b = self.rows(ab, i)
        return self.wq.at[l, pl.ds(pl.multiple_of(a + b, 16), 16), :]
    def slh(self, l, ab, i, h):
        a, b = self.rows(ab, i)
        return self.wq.at[l, pl.ds(pl.multiple_of(a + b, 16), 16), pl.ds(h * 1536, 1536)]
    def blk(self, l, ab, k):
        a, _ = self.rows(ab, 0, k)
        return self.wq.at[l, pl.ds(pl.multiple_of(a, 64), 64), :]
    def blkh(self, l, ab, k, h):
        a, _ = self.rows(ab, 0, k)
        return self.wq.at[l, pl.ds(pl.multiple_of(a + h * 32, 32), 32), :]
    def wop(self, l, h):
        return self.wo.at[l, pl.ds(pl.multiple_of(self.c * 512 + h * 256, 256), 256), :]
    def layer_of(self, d):
        return lax.rem(self.x + d, 4)
    def stage_layer(self, j):
        return j + (self.x <= j).astype(jnp.int32)
    def start_x(self):
        x = self.x
        for ab in (0, 1):
            a, b = self.rows(ab, 0)
            src = self.wq_in.at[0, pl.ds(pl.multiple_of(a + b, 16), 16), :]
            for dx, d in (((1, 3), (-1, 1)) if ab == 0 else ((-1, 1), (1, 3))):
                self.send(src, self.sl(x, ab, 0), self.xs.at[ab, d - 1], self.xr.at[ab, d - 1], self.dev(dx=dx))
    def start_x_wo(self):
        for n in (0, 1):
            for dx, d, h in ((1, 3, n), (-1, 1, 1 - n)):
                src = self.wo_in.at[0, pl.ds(pl.multiple_of(self.c * 512 + h * 256, 256), 256), :]
                self.send(src, self.wop(self.x, h), self.xs.at[2 + h, d - 1], self.xr.at[2 + h, d - 1], self.dev(dx=dx))
    def start_own(self):
        pltpu.make_async_copy(self.wq_in.at[0], self.wq.at[self.x], self.own.at[0]).start()
        pltpu.make_async_copy(self.wo_in.at[0], self.wo.at[self.x], self.own.at[1]).start()
    def wait_own(self):
        pltpu.make_async_copy(self.wq_in.at[0], self.wq.at[self.x], self.own.at[0]).wait()
        pltpu.make_async_copy(self.wo_in.at[0], self.wo.at[self.x], self.own.at[1]).wait()
    def x_forward_qkv(self):
        for ab, d, dx in ((0, 3, 1), (1, 1, -1)):
            l = self.layer_of(d)
            self.recv(self.sl(l, ab, 0), self.xs.at[ab, d - 1], self.xr.at[ab, d - 1])
            self.send(self.sl(l, ab, 0), self.sl(l, ab, 0), self.xs.at[ab, 1], self.xr.at[ab, 1], self.dev(dx=dx))
    def x_wait(self):
        for ab, d in ((0, 1), (1, 3), (0, 2), (1, 2)):
            self.recv(self.sl(self.layer_of(d), ab, 0), self.xs.at[ab, d - 1], self.xr.at[ab, d - 1])
    def dd_send(self, ref, a, b):
        if self.use_dd:
            self.send(ref, ref, self.ds.at[a, b], self.dr.at[a, b], self.dev(dc=1))
    def x_wo_forward(self):
        for h, d, dx in ((0, 3, 1), (1, 1, -1)):
            l = self.layer_of(d)
            r = self.wop(l, h)
            self.recv(r, self.xs.at[2 + h, d - 1], self.xr.at[2 + h, d - 1])
            self.send(r, r, self.xs.at[2 + h, 1], self.xr.at[2 + h, 1], self.dev(dx=dx))
            self.dd_send(r, 8 + h, d - 1)
    def x_wo_rest(self):
        for h, d in ((0, 1), (1, 3), (0, 2), (1, 2)):
            r = self.wop(self.layer_of(d), h)
            self.recv(r, self.xs.at[2 + h, d - 1], self.xr.at[2 + h, d - 1])
            self.dd_send(r, 8 + h, d - 1)
    def ax(self, phase, ab, s):
        if (phase == 1) == (ab == 0):
            return self.dev(dy=s)
        return self.dev(dz=s)
    def p1s1(self, j):
        l = self.stage_layer(j)
        for n in (0, 1):
            for k, s in enumerate((1, -1)):
                for ab in (0, 1):
                    h = k if n == 0 else 1 - k
                    r = self.slh(l, ab, 0, h)
                    self.send(r, r, self.p1s.at[ab, 2 * n + k, j], self.p1r.at[ab, 2 * n + k, j], self.ax(1, ab, s))
    def p1s2(self, j):
        l = self.stage_layer(j)
        for k, s in enumerate((1, -1)):
            for ab in (0, 1):
                r = self.slh(l, ab, -s, k)
                self.recv(r, self.p1s.at[ab, k, j], self.p1r.at[ab, k, j])
                self.send(r, r, self.p1s.at[ab, 4 + k, j], self.p1r.at[ab, 4 + k, j], self.ax(1, ab, s))
    def p2s1(self, j):
        l = self.stage_layer(j)
        for ab in (0, 1):
            for k, s in enumerate((1, -1)):
                self.recv(self.slh(l, ab, -s, 1 - k), self.p1s.at[ab, 2 + k, j], self.p1r.at[ab, 2 + k, j])
                self.recv(self.slh(l, ab, 2, k), self.p1s.at[ab, 4 + k, j], self.p1r.at[ab, 4 + k, j])
        for n in (0, 1):
            for k, s in enumerate((1, -1)):
                for ab in (0, 1):
                    h = k if n == 0 else 1 - k
                    r = self.blkh(l, ab, 0, h)
                    self.send(r, r, self.p2s.at[ab, 2 * n + k, j], self.p2r.at[ab, 2 * n + k, j], self.ax(2, ab, s))
        for ab in (0, 1):
            self.dd_send(self.blk(l, ab, 0), ab * 4, j)
    def p2s2(self, j):
        l = self.stage_layer(j)
        for k, s in enumerate((1, -1)):
            for ab in (0, 1):
                r = self.blkh(l, ab, -s, k)
                self.recv(r, self.p2s.at[ab, k, j], self.p2r.at[ab, k, j])
                self.send(r, r, self.p2s.at[ab, 4 + k, j], self.p2r.at[ab, 4 + k, j], self.ax(2, ab, s))
    def fin(self, j):
        l = self.stage_layer(j)
        for ab in (0, 1):
            for k, s in enumerate((1, -1)):
                self.recv(self.blkh(l, ab, -s, 1 - k), self.p2s.at[ab, 2 + k, j], self.p2r.at[ab, 2 + k, j])
                self.dd_send(self.blk(l, ab, -s), ab * 4 + 1 + k, j)
        for ab in (0, 1):
            for k in (0, 1):
                self.recv(self.blkh(l, ab, 2, k), self.p2s.at[ab, 4 + k, j], self.p2r.at[ab, 4 + k, j])
            self.dd_send(self.blk(l, ab, 2), ab * 4 + 3, j)
    def other(self):
        g = Gather.__new__(Gather)
        g.__dict__.update(self.__dict__)
        g.c = 1 - self.c
        return g
    def dd_wait_qkv(self, j):
        if not self.use_dd: return
        g = self.other()
        l = self.stage_layer(j)
        for ab in (0, 1):
            for n, k in ((0, 0), (1, -1), (2, 1), (3, 2)):
                self.recv(g.blk(l, ab, k), self.ds.at[ab * 4 + n, j], self.dr.at[ab * 4 + n, j])
    def dd_wait_wo(self, d):
        if not self.use_dd: return
        g = self.other()
        for h in (0, 1):
            self.recv(g.wop(self.layer_of(d), h), self.ds.at[8 + h, d - 1], self.dr.at[8 + h, d - 1])
    def drain(self):
        for cp in self.pending:
            cp.wait_send()

SEMS = [pltpu.SemaphoreType.DMA((4, 3)), pltpu.SemaphoreType.DMA((4, 3)),
        pltpu.SemaphoreType.DMA((2, 6, 3)), pltpu.SemaphoreType.DMA((2, 6, 3)),
        pltpu.SemaphoreType.DMA((2, 6, 3)), pltpu.SemaphoreType.DMA((2, 6, 3)),
        pltpu.SemaphoreType.DMA((10, 3)), pltpu.SemaphoreType.DMA((10, 3)),
        pltpu.SemaphoreType.DMA((2,))]


def gather_kernel(wq_in, wo_in, oq, oo, wq, wo, *sems):
    g = Gather(wq_in, wo_in, wq, wo, sems)
    g.barrier()
    g.start_x()
    g.start_own()
    g.x_forward_qkv()
    g.start_x_wo()
    g.x_wait()
    g.p1s1(0)
    g.p1s1(1)
    g.p1s2(0)
    g.p2s1(0)
    g.p1s2(1)
    g.p2s2(0)
    g.p1s1(2)
    g.p2s1(1)
    g.fin(0)
    g.p1s2(2)
    g.p2s2(1)
    g.x_wo_forward()
    g.p2s1(2)
    g.fin(1)
    g.p2s2(2)
    g.x_wo_rest()
    g.fin(2)
    for j in range(3): g.dd_wait_qkv(j)
    for d in (1, 2, 3): g.dd_wait_wo(d)
    g.wait_own()
    g.drain()
    a = pltpu.make_async_copy(wq, oq, sems[-1].at[0])
    b = pltpu.make_async_copy(wo, oo, sems[-1].at[1])
    a.start()
    b.start()
    a.wait()
    b.wait()


def gather(wq, wo):
    return pl.pallas_call(
        gather_kernel,
        out_shape=(
            jax.ShapeDtypeStruct((4, 1024, 3072), jnp.bfloat16),
            jax.ShapeDtypeStruct((4, 1024, 1024), jnp.bfloat16),
        ),
        in_specs=[pl.BlockSpec(memory_space=pl.ANY)] * 2,
        out_specs=[pl.BlockSpec(memory_space=pl.ANY)] * 2,
        scratch_shapes=[
            pltpu.VMEM((4, 1024, 3072), jnp.bfloat16),
            pltpu.VMEM((4, 1024, 1024), jnp.bfloat16),
        ]
        + SEMS,
        compiler_params=pltpu.CompilerParams(
            collective_id=0, has_side_effects=True, vmem_limit_bytes=60 * 1024 * 1024
        ),
    )(wq, wo)


def scaled_norm(volume, gain_row):
    values = volume.astype(jnp.float32)
    mean_square = jnp.mean(values * values, axis=-1, keepdims=True)
    return (values * lax.rsqrt(mean_square + 1e-06) * gain_row).astype(jnp.bfloat16)


def attention_layer(volume, gain_row, qkv_mat, out_mat, causal):
    extent_a, length, extent_c, features = volume.shape
    head_size = features // HEADS
    normed = scaled_norm(volume, gain_row)
    packed = jnp.dot(normed.reshape(-1, features), qkv_mat, preferred_element_type=jnp.float32)
    packed = packed.astype(jnp.bfloat16).reshape(extent_a, length, extent_c, 3, HEADS, head_size)
    queries = packed[:, :, :, 0]
    key_rows = packed[:, :, :, 1]
    values = packed[:, :, :, 2]
    scores = jnp.einsum(
        "alchd,amchd->achlm", queries, key_rows, preferred_element_type=jnp.float32
    ) * head_size ** (-0.5)
    if causal:
        allowed = jnp.arange(length)[:, None] >= jnp.arange(length)[None, :]
        scores = jnp.where(allowed, scores, -1e30)
    weights = jax.nn.softmax(scores, axis=-1).astype(jnp.bfloat16)
    context = jnp.einsum("achlm,amchd->alchd", weights, values, preferred_element_type=jnp.float32)
    context = context.astype(jnp.bfloat16).reshape(-1, features)
    update = jnp.dot(context, out_mat, preferred_element_type=jnp.float32).reshape(volume.shape)
    return (volume.astype(jnp.float32) + update).astype(jnp.bfloat16)


def owner_table(owner, peers, max_rows):
    rows_all = owner.shape[0]
    position = jnp.arange(rows_all, dtype=jnp.int32)
    alike = (owner[:, None] == owner[None, :]) & (position[:, None] < position[None, :])
    slot_of = jnp.sum(alike.astype(jnp.int32), axis=0)
    device_ids = jnp.arange(peers, dtype=jnp.int32)
    slot_ids = jnp.arange(max_rows, dtype=jnp.int32)
    match = (owner[None, None, :] == device_ids[:, None, None]) & (
        slot_of[None, None, :] == slot_ids[None, :, None]
    )
    chosen = jnp.sum(jnp.where(match, position[None, None, :], 0), axis=2).reshape(-1)
    present = jnp.any(match, axis=2).reshape(-1)
    return (chosen, present)


def pick_rows(lines_volume, chosen, present, peers, max_rows):
    lines_dev, img_rows, features = lines_volume.shape
    picked = jnp.take(lines_volume, chosen, axis=1)
    picked = jnp.where(present[None, :, None], picked, jnp.zeros((), jnp.bfloat16))
    return picked.reshape(lines_dev, peers, max_rows, features)


def local(frames_in, order, owner, qkv_weight, out_weight, gains):
    sections = lax.axis_size("section")
    peers = lax.axis_size("seq")
    section = lax.axis_index("section")
    clips, lines_dev, img_rows, features = frames_in.shape
    lines_all = lines_dev * peers
    columns = lines_all // FRAMES
    max_rows = 2 * img_rows // peers
    wq, wo = gather(qkv_weight, out_weight)
    gains = lax.all_gather(gains, "section", axis=0, tiled=True)
    chosen, present = owner_table(owner, peers, max_rows)
    clip = lax.dynamic_index_in_dim(frames_in, order[sections - 1 - section], 0, keepdims=False)
    mixed = attention_layer(clip[:, :, None, :], gains[0], wq[0], wo[0], False)[:, :, 0, :]
    owned = pick_rows(mixed, chosen, present, peers, max_rows)
    v = lax.all_to_all(owned, "seq", split_axis=1, concat_axis=0, tiled=True)
    v = attention_layer(v.reshape(1, FRAMES, columns * max_rows, features), gains[1], wq[1], wo[1], False)
    for layer in (2, 3):
        v = v.reshape(FRAMES, columns, max_rows, features)
        v = attention_layer(v, gains[layer], wq[layer], wo[layer], True)
    return v.reshape(1, lines_all, max_rows, features)


def solution(mesh):
    placed = (
        P(None, "seq", None, None),
        P(),
        P(),
        P("section", None, None),
        P("section", None, None),
        P("section", None),
    )
    return jax.shard_map(
        local,
        mesh=mesh,
        in_specs=placed,
        out_specs=P("section", None, "seq", None),
        check_vma=False,
    )
```

```python
import functools

import jax
import jax.numpy as jnp
from jax import lax
from jax.experimental import pallas as pl
from jax.experimental.pallas import tpu as pltpu
from jax.sharding import PartitionSpec as P

MESH = pl.DeviceIdType.MESH
HEADS = 16
F32, BF = jnp.float32, jnp.bfloat16


class Gather:
    def __init__(self, wq_in, wo_in, wq, wo, sems):
        self.wq_in, self.wo_in, self.wq, self.wo = wq_in, wo_in, wq, wo
        (self.xs, self.xr, self.p1s, self.p1r, self.p2s, self.p2r) = sems[:6]
        (self.ds, self.dr, self.gs, self.gr, self.es, self.er, self.own) = sems[6:]
        self.x = lax.axis_index("section")
        self.q = lax.axis_index("seq")
        self.c = lax.rem(self.q, 2)
        self.y = lax.rem(self.q // 2, 4)
        self.z = self.q // 8
        self.pending = []

    def dev(self, dx=0, dy=0, dz=0, dc=0):
        x = lax.rem(self.x + (dx + 4), 4)
        y = lax.rem(self.y + (dy + 4), 4)
        z = lax.rem(self.z + (dz + 4), 4)
        c = lax.rem(self.c + dc, 2)
        return (x, (z * 4 + y) * 2 + c)
    def peer(self, k):
        return self.dev(0, lax.rem(k // 2, 4), k // 8, lax.rem(k, 2))

    def source(self, k):
        return self.dev(0, 4 - lax.rem(k // 2, 4), 4 - k // 8, 2 - lax.rem(k, 2))[1]

    def barrier(self):
        sem = pltpu.get_barrier_semaphore()
        for dx in (1, 2, 3):
            pl.semaphore_signal(sem, inc=1, device_id=self.dev(dx=dx), device_id_type=MESH)

        @pl.loop(1, 32)
        def _(k):
            pl.semaphore_signal(sem, inc=1, device_id=self.peer(k), device_id_type=MESH)

        pl.semaphore_wait(sem, 34)

    def copy(self, src, dst, ss, rs, dev):
        return pltpu.make_async_remote_copy(src_ref=src, dst_ref=dst, send_sem=ss, recv_sem=rs, device_id=dev, device_id_type=MESH)
    def send(self, src, dst, ss, rs, dev):
        cp = self.copy(src, dst, ss, rs, dev)
        cp.start()
        self.pending.append(cp)
    def recv(self, dst, ss, rs):
        self.copy(dst, dst, ss, rs, self.dev(dc=1)).wait_recv()
    def rows(self, ab, i=0, blk=0):
        y, z = self.y, self.z
        if ab == 0:
            major, minor = lax.rem(z + (blk + 4), 4), lax.rem(y + (i + 4), 4)
        else:
            major, minor = lax.rem(y + (blk + 4), 4), lax.rem(z + (i + 4), 4)
        return self.c * 512 + ab * 256 + major * 64, minor * 16
    def sl(self, l, ab, i):
        a, b = self.rows(ab, i)
        return self.wq.at[l, pl.ds(pl.multiple_of(a + b, 16), 16), :]
    def slh(self, l, ab, i, h):
        a, b = self.rows(ab, i)
        return self.wq.at[l, pl.ds(pl.multiple_of(a + b, 16), 16), pl.ds(h * 1536, 1536)]
    def blk(self, l, ab, k):
        a, _ = self.rows(ab, 0, k)
        return self.wq.at[l, pl.ds(pl.multiple_of(a, 64), 64), :]
    def blkh(self, l, ab, k, h):
        a, _ = self.rows(ab, 0, k)
        return self.wq.at[l, pl.ds(pl.multiple_of(a + h * 32, 32), 32), :]
    def wop(self, l, h):
        return self.wo.at[l, pl.ds(pl.multiple_of(self.c * 512 + h * 256, 256), 256), :]
    def layer_of(self, d):
        return lax.rem(self.x + d, 4)
    def stage_layer(self, j):
        return j + (self.x <= j).astype(jnp.int32)
    def start_x(self):
        x = self.x
        for ab in (0, 1):
            a, b = self.rows(ab, 0)
            src = self.wq_in.at[0, pl.ds(pl.multiple_of(a + b, 16), 16), :]
            for dx, d in (((1, 3), (-1, 1)) if ab == 0 else ((-1, 1), (1, 3))):
                self.send(src, self.sl(x, ab, 0), self.xs.at[ab, d - 1], self.xr.at[ab, d - 1], self.dev(dx=dx))
    def wo_own(self, second):
        copies = []
        for dx, d, h in ((1, 3, second), (-1, 1, 1 - second)):
            src = self.wo_in.at[0, pl.ds(pl.multiple_of(self.c * 512 + h * 256, 256), 256), :]
            sems = self.xs.at[2 + h, d - 1], self.xr.at[2 + h, d - 1]
            copies.append(self.copy(src, self.wop(self.x, h), *sems, self.dev(dx=dx)))
        return copies

    def wo_first(self):
        for cp in self.wo_own(0):
            cp.start()
            self.pending.append(cp)
        second = self.wo_own(1)
        self.pending.extend(second)

        @pl.when(self.x == 0)
        def _():
            for cp in second:
                cp.start()

    def wo_forward(self):
        for h, d, dx in ((0, 3, 1), (1, 1, -1)):
            r = self.wop(self.layer_of(d), h)
            self.recv(r, self.xs.at[2 + h, d - 1], self.xr.at[2 + h, d - 1])
            self.send(r, r, self.xs.at[2 + h, 1], self.xr.at[2 + h, 1], self.dev(dx=dx))
            self.dd_send(r, 8 + h, d - 1)

        @pl.when(self.x != 0)
        def _():
            for cp in self.wo_own(1):
                cp.start()

    def wo_ready(self, layer):
        dist = lax.rem(layer - self.x + 4, 4)
        for d, hs in ((1, (0,)), (2, (0, 1)), (3, (1,))):
            if layer == 0:
                for h in hs:
                    r = self.wop(self.layer_of(d), h)
                    self.pending.append(
                        self.copy(r, r, self.ds.at[8 + h, d - 1], self.dr.at[8 + h, d - 1], self.dev(dc=1))
                    )

            @pl.when(dist == d)
            def _():
                for h in hs:
                    r = self.wop(self.layer_of(d), h)
                    self.recv(r, self.xs.at[2 + h, d - 1], self.xr.at[2 + h, d - 1])
                    self.copy(r, r, self.ds.at[8 + h, d - 1], self.dr.at[8 + h, d - 1], self.dev(dc=1)).start()
                g = self.other()
                for h in (0, 1):
                    self.recv(g.wop(self.layer_of(d), h), self.ds.at[8 + h, d - 1], self.dr.at[8 + h, d - 1])

    def gains_start(self, g_in, g_all):
        for dx in (1, 2, 3):
            self.send(g_in, g_all.at[self.x], self.gs.at[dx - 1], self.gr.at[dx - 1], self.dev(dx=dx))

    def gains_wait(self, g_all):
        for dx in (1, 2, 3):
            self.recv(g_all.at[self.layer_of(4 - dx)], self.gs.at[dx - 1], self.gr.at[dx - 1])

    def exchange_copy(self, k, send, land):
        src = send.at[pl.ds(pl.multiple_of(self.peer(k)[1] * 16, 16), 16), :]
        dst = land.at[pl.ds(pl.multiple_of(self.q * 16, 16), 16), :]
        return self.copy(src, dst, self.es.at[k], self.er.at[k], self.peer(k))

    def exchange_start(self, send, land):
        @pl.loop(1, 32)
        def _(k):
            self.exchange_copy(k, send, land).start()

        rows = pl.ds(pl.multiple_of(self.q * 16, 16), 16)
        pltpu.make_async_copy(send.at[rows, :], land.at[rows, :], self.es.at[0]).start()

    def exchange_wait(self, send, land):
        @pl.loop(1, 32)
        def _(k):
            rows = pl.ds(pl.multiple_of(self.source(k) * 16, 16), 16)
            self.recv(land.at[rows, :], self.es.at[k], self.er.at[k])

        rows = pl.ds(pl.multiple_of(self.q * 16, 16), 16)
        pltpu.make_async_copy(send.at[rows, :], land.at[rows, :], self.es.at[0]).wait()

    def exchange_drain(self, send, land):
        @pl.loop(1, 32)
        def _(k):
            self.exchange_copy(k, send, land).wait_send()

    def own_copies(self, frames_in, frames, g_in, g_all):
        return [
            pltpu.make_async_copy(frames_in, frames, self.own.at[0]),
            pltpu.make_async_copy(g_in, g_all.at[self.x], self.own.at[1]),
            pltpu.make_async_copy(self.wq_in.at[0], self.wq.at[self.x], self.own.at[2]),
            pltpu.make_async_copy(self.wo_in.at[0], self.wo.at[self.x], self.own.at[3]),
        ]

    def x_forward_qkv(self):
        for ab, d, dx in ((0, 3, 1), (1, 1, -1)):
            l = self.layer_of(d)
            self.recv(self.sl(l, ab, 0), self.xs.at[ab, d - 1], self.xr.at[ab, d - 1])
            self.send(self.sl(l, ab, 0), self.sl(l, ab, 0), self.xs.at[ab, 1], self.xr.at[ab, 1], self.dev(dx=dx))
    def x_wait(self):
        for ab, d in ((0, 1), (1, 3), (0, 2), (1, 2)):
            self.recv(self.sl(self.layer_of(d), ab, 0), self.xs.at[ab, d - 1], self.xr.at[ab, d - 1])
    def dd_send(self, ref, a, b):
        self.send(ref, ref, self.ds.at[a, b], self.dr.at[a, b], self.dev(dc=1))

    def ax(self, phase, ab, s):
        if (phase == 1) == (ab == 0):
            return self.dev(dy=s)
        return self.dev(dz=s)
    def p1s1(self, j):
        l = self.stage_layer(j)
        for n in (0, 1):
            for k, s in enumerate((1, -1)):
                for ab in (0, 1):
                    h = k if n == 0 else 1 - k
                    r = self.slh(l, ab, 0, h)
                    self.send(r, r, self.p1s.at[ab, 2 * n + k, j], self.p1r.at[ab, 2 * n + k, j], self.ax(1, ab, s))
    def p1s2(self, j):
        l = self.stage_layer(j)
        for k, s in enumerate((1, -1)):
            for ab in (0, 1):
                r = self.slh(l, ab, -s, k)
                self.recv(r, self.p1s.at[ab, k, j], self.p1r.at[ab, k, j])
                self.send(r, r, self.p1s.at[ab, 4 + k, j], self.p1r.at[ab, 4 + k, j], self.ax(1, ab, s))
    def p2s1(self, j):
        l = self.stage_layer(j)
        for ab in (0, 1):
            for k, s in enumerate((1, -1)):
                self.recv(self.slh(l, ab, -s, 1 - k), self.p1s.at[ab, 2 + k, j], self.p1r.at[ab, 2 + k, j])
                self.recv(self.slh(l, ab, 2, k), self.p1s.at[ab, 4 + k, j], self.p1r.at[ab, 4 + k, j])
        for n in (0, 1):
            for k, s in enumerate((1, -1)):
                for ab in (0, 1):
                    h = k if n == 0 else 1 - k
                    r = self.blkh(l, ab, 0, h)
                    self.send(r, r, self.p2s.at[ab, 2 * n + k, j], self.p2r.at[ab, 2 * n + k, j], self.ax(2, ab, s))
        for ab in (0, 1):
            self.dd_send(self.blk(l, ab, 0), ab * 4, j)
    def p2s2(self, j):
        l = self.stage_layer(j)
        for k, s in enumerate((1, -1)):
            for ab in (0, 1):
                r = self.blkh(l, ab, -s, k)
                self.recv(r, self.p2s.at[ab, k, j], self.p2r.at[ab, k, j])
                self.send(r, r, self.p2s.at[ab, 4 + k, j], self.p2r.at[ab, 4 + k, j], self.ax(2, ab, s))
    def fin(self, j):
        l = self.stage_layer(j)
        for ab in (0, 1):
            for k, s in enumerate((1, -1)):
                self.recv(self.blkh(l, ab, -s, 1 - k), self.p2s.at[ab, 2 + k, j], self.p2r.at[ab, 2 + k, j])
                self.dd_send(self.blk(l, ab, -s), ab * 4 + 1 + k, j)
        for ab in (0, 1):
            for k in (0, 1):
                self.recv(self.blkh(l, ab, 2, k), self.p2s.at[ab, 4 + k, j], self.p2r.at[ab, 4 + k, j])
            self.dd_send(self.blk(l, ab, 2), ab * 4 + 3, j)
    def other(self):
        g = Gather.__new__(Gather)
        g.__dict__.update(self.__dict__)
        g.c = 1 - self.c
        return g
    def qkv_ready(self, j):
        g = self.other()
        l = self.stage_layer(j)
        for ab in (0, 1):
            for n, k in ((0, 0), (1, -1), (2, 1), (3, 2)):
                self.recv(g.blk(l, ab, k), self.ds.at[ab * 4 + n, j], self.dr.at[ab * 4 + n, j])

    def drain(self):
        for cp in self.pending:
            cp.wait_send()


def norm_into(x_ref, gain, h_ref, m):
    @pl.loop(0, m // 64)
    def _(i):
        r = pl.ds(pl.multiple_of(i * 64, 64), 64)
        v = x_ref[r, :].astype(F32)
        ms = jnp.mean(v * v, axis=-1, keepdims=True)
        h_ref[r, :] = (v * lax.rsqrt(ms + 1e-06) * gain).astype(BF)

def qkv_into(h_ref, w_ref, qkv_ref, m, tn=512):
    @pl.loop(0, 3072 // tn)
    def _(i):
        cidx = pl.ds(pl.multiple_of(i * tn, tn), tn)
        qkv_ref[pl.ds(0, m), cidx] = jnp.dot(h_ref[pl.ds(0, m), :], w_ref[:, cidx], preferred_element_type=F32).astype(BF)

def out_into(ctx_ref, w_ref, x_ref, y_ref, m, tn=256):
    @pl.loop(0, 1024 // tn)
    def _(i):
        cidx = pl.ds(pl.multiple_of(i * tn, tn), tn)
        u = jnp.dot(ctx_ref[pl.ds(0, m), :], w_ref[:, cidx], preferred_element_type=F32)
        y_ref[pl.ds(0, m), cidx] = (x_ref[pl.ds(0, m), cidx].astype(F32) + u).astype(BF)

def attend(q2, k2, v2, mask, lo, ind):
    z = jnp.zeros((), BF)
    kk = jnp.concatenate([jnp.where(lo, k2, z), jnp.where(lo, z, k2)], axis=0)
    vv = jnp.concatenate([jnp.where(lo, v2, z), jnp.where(lo, z, v2)], axis=0)
    vv = jnp.concatenate([vv, ind], axis=1)
    s = lax.dot_general(q2, kk, (((1,), (1,)), ((), ())), preferred_element_type=F32)
    if mask is not None:
        s = jnp.where(mask, s, -1e30)
    halves = []
    for n in (0, 1):
        t = s[:, n * 128:n * 128 + 128]
        t = jnp.exp2((t - jnp.max(t, axis=-1, keepdims=True)) * 0.18033688011112042)
        halves.append(t.astype(BF))
    o = jnp.dot(jnp.concatenate(halves, axis=1), vv, preferred_element_type=F32)
    return (o[:, :128] / o[:, 128:]).astype(BF)

def attention_into(kind, qkv_ref, ctx_ref, blocks, pairs=1):
    lo = lax.broadcasted_iota(jnp.int32, (128, 128), 1) < 64
    one, z = jnp.ones((), BF), jnp.zeros((), BF)
    ind = jnp.concatenate([jnp.where(lo, one, z), jnp.where(lo, z, one)], axis=0)
    i = lax.broadcasted_iota(jnp.int32, (128, 256), 0)
    j = lax.rem(lax.broadcasted_iota(jnp.int32, (128, 256), 1), 128)
    mask = None
    if kind == "frame":
        mask = lax.rem(i, 32) == lax.rem(j, 32)
    if kind == "row":
        mask = (lax.rem(i, 8) == lax.rem(j, 8)) & (i >= j)
    @pl.loop(0, HEADS // 2 // pairs)
    def _(step):
        for p in range(pairs):
            for b in range(blocks):
                first = (step * pairs + p) * 128

                def get(base):
                    c = pl.ds(pl.multiple_of(base + first, 128), 128)
                    if kind == "frame":
                        parts = [qkv_ref[pl.ds(f * 128 + b * 32, 32), c] for f in range(4)]
                        return jnp.concatenate(parts, axis=0)
                    return qkv_ref[pl.ds(b * 128, 128), c]

                o = attend(get(0), get(1024), get(2048), mask, lo, ind)
                c = pl.ds(pl.multiple_of(first, 128), 128)
                if kind == "frame":
                    for f in range(4):
                        ctx_ref[pl.ds(f * 128 + b * 32, 32), c] = o[f * 32 : f * 32 + 32]
                else:
                    ctx_ref[pl.ds(b * 128, 128), c] = o


def select_matrix(owner_row, owner_col, pick_ref):
    before = lax.broadcasted_iota(jnp.int32, (128, 128), 0) < lax.broadcasted_iota(jnp.int32, (128, 128), 1)
    alike = (owner_col == owner_row) & before
    slot = jnp.sum(jnp.where(alike, 1.0, 0.0), axis=0, keepdims=True)
    code = owner_row.astype(F32) * 8.0 + slot
    code = jnp.concatenate([code, code], axis=1)
    k = lax.broadcasted_iota(jnp.int32, (512, 256), 0)
    r = lax.broadcasted_iota(jnp.int32, (512, 256), 1)
    want = ((k // 16) * 8 + lax.rem(k, 8)).astype(F32)
    hit = (code == want) & (lax.rem(k // 8, 2) == r // 128)
    pick_ref[...] = jnp.where(hit, 1.0, 0.0).astype(BF)


def kernel(
    order, frames_in, owner_row, owner_col, wq_in, wo_in, g_in, out,
    wq, wo, g_all, frames, clip, pick, send, vol, h, qkv, *sems
):
    g = Gather(wq_in, wo_in, wq, wo, sems)
    g.barrier()
    g.start_x()
    own = g.own_copies(frames_in, frames, g_in, g_all)
    for cp in own:
        cp.start()
    g.gains_start(g_in, g_all)
    g.x_forward_qkv()
    g.wo_first()
    g.x_wait()
    g.p1s1(0)
    g.p1s1(1)
    select_matrix(owner_row[...], owner_col[...], pick)
    g.p1s2(0)
    g.p2s1(0)
    g.p1s2(1)
    own[0].wait()
    turn = order[3 - g.x]
    clip[...] = frames[turn].reshape(256, 1024)
    own[1].wait()
    g.gains_wait(g_all)
    norm_into(clip, g_all[0], h, 256)
    g.p2s2(0)
    g.wo_forward()
    g.p1s1(2)
    g.p2s1(1)
    g.fin(0)
    own[2].wait()
    own[3].wait()
    g.qkv_ready(0)
    qkv_into(h, wq.at[0], qkv, 256)
    g.p1s2(2)
    g.p2s2(1)
    attention_into("column", qkv, h, 2, 2)
    g.wo_ready(0)
    out_into(h, wo.at[0], clip, clip, 256)

    @pl.loop(0, 4)
    def _(i):
        c = pl.ds(pl.multiple_of(i * 256, 256), 256)
        send[:, c] = jnp.dot(pick[...], clip[:, c], preferred_element_type=F32).astype(BF)

    g.exchange_start(send, vol)
    g.p2s1(2)
    g.fin(1)
    g.qkv_ready(1)
    g.exchange_wait(send, vol)
    norm_into(vol, g_all[1], h, 512)
    qkv_into(h, wq.at[1], qkv, 512)
    g.p2s2(2)
    attention_into("frame", qkv, h, 4)
    g.wo_ready(1)
    out_into(h, wo.at[1], vol, vol, 512)
    g.fin(2)
    g.qkv_ready(2)
    g.wo_ready(2)
    g.wo_ready(3)
    for l in (2, 3):
        norm_into(vol, g_all[l], h, 512)
        qkv_into(h, wq.at[l], qkv, 512)
        attention_into("row", qkv, h, 4)
        out_into(h, wo.at[l], vol, out if l == 3 else vol, 512)
    g.exchange_drain(send, vol)
    g.drain()


def local(frames_in, order, owner, qkv_weight, out_weight, gains):
    vmem = pl.BlockSpec(memory_space=pltpu.VMEM)
    hbm = pl.BlockSpec(memory_space=pl.ANY)
    dma = pltpu.SemaphoreType.DMA
    result = pl.pallas_call(
        kernel,
        out_shape=jax.ShapeDtypeStruct((512, 1024), BF),
        in_specs=[pl.BlockSpec(memory_space=pltpu.SMEM), hbm, vmem, vmem, hbm, hbm, hbm],
        out_specs=vmem,
        scratch_shapes=[
            pltpu.VMEM((4, 1024, 3072), BF),
            pltpu.VMEM((4, 1024, 1024), BF),
            pltpu.VMEM((4, 1, 1024), F32),
            pltpu.VMEM((4, 2, 128, 1024), BF),
            pltpu.VMEM((256, 1024), BF),
            pltpu.VMEM((512, 256), BF),
            pltpu.VMEM((512, 1024), BF),
            pltpu.VMEM((512, 1024), BF),
            pltpu.VMEM((512, 1024), BF),
            pltpu.VMEM((512, 3072), BF),
            dma((4, 3)), dma((4, 3)),
            dma((2, 6, 3)), dma((2, 6, 3)),
            dma((2, 6, 3)), dma((2, 6, 3)),
            dma((10, 3)), dma((10, 3)),
            dma((3,)), dma((3,)),
            dma((32,)), dma((32,)),
            dma((4,)),
        ],
        compiler_params=pltpu.CompilerParams(
            collective_id=0, has_side_effects=True, vmem_limit_bytes=60 * 1024 * 1024
        ),
    )(order, frames_in, owner[None, :], owner[:, None], qkv_weight, out_weight, gains)
    return result.reshape(1, 64, 8, 1024)


def solution(mesh):
    placed = (
        P(None, "seq", None, None),
        P(),
        P(),
        P("section", None, None),
        P("section", None, None),
        P("section", None),
    )
    return jax.shard_map(
        local,
        mesh=mesh,
        in_specs=placed,
        out_specs=P("section", None, "seq", None),
        check_vma=False,
    )
```

```python
import functools

import jax
import jax.numpy as jnp
from jax import lax
from jax.experimental import pallas as pl
from jax.experimental.pallas import tpu as pltpu
from jax.sharding import PartitionSpec as P

MESH = pl.DeviceIdType.MESH
HEADS = 16
F32, BF = jnp.float32, jnp.bfloat16


class Gather:
    def __init__(self, wq_in, wo_in, wq, wo, sems):
        self.wq_in, self.wo_in, self.wq, self.wo = wq_in, wo_in, wq, wo
        (self.xs, self.xr, self.p1s, self.p1r, self.p2s, self.p2r) = sems[:6]
        (self.ds, self.dr, self.gs, self.gr, self.es, self.er, self.own) = sems[6:]
        self.x = lax.axis_index("section")
        self.q = lax.axis_index("seq")
        self.c = lax.rem(self.q, 2)
        self.y = lax.rem(self.q // 2, 4)
        self.z = self.q // 8
        self.pending = []

    def dev(self, dx=0, dy=0, dz=0, dc=0):
        x = lax.rem(self.x + (dx + 4), 4)
        y = lax.rem(self.y + (dy + 4), 4)
        z = lax.rem(self.z + (dz + 4), 4)
        c = lax.rem(self.c + dc, 2)
        return (x, (z * 4 + y) * 2 + c)
    def peer(self, k):
        return self.dev(0, lax.rem(k // 2, 4), k // 8, lax.rem(k, 2))

    def source(self, k):
        return self.dev(0, 4 - lax.rem(k // 2, 4), 4 - k // 8, 2 - lax.rem(k, 2))[1]

    def barrier(self):
        sem = pltpu.get_barrier_semaphore()
        for dx in (1, 2, 3):
            pl.semaphore_signal(sem, inc=1, device_id=self.dev(dx=dx), device_id_type=MESH)

        @pl.loop(1, 32)
        def _(k):
            pl.semaphore_signal(sem, inc=1, device_id=self.peer(k), device_id_type=MESH)

        pl.semaphore_wait(sem, 34)

    def copy(self, src, dst, ss, rs, dev):
        return pltpu.make_async_remote_copy(src_ref=src, dst_ref=dst, send_sem=ss, recv_sem=rs, device_id=dev, device_id_type=MESH)
    def send(self, src, dst, ss, rs, dev):
        cp = self.copy(src, dst, ss, rs, dev)
        cp.start()
        self.pending.append(cp)
    def recv(self, dst, ss, rs):
        self.copy(dst, dst, ss, rs, self.dev(dc=1)).wait_recv()
    def rows(self, ab, i=0, blk=0):
        y, z = self.y, self.z
        if ab == 0:
            major, minor = lax.rem(z + (blk + 4), 4), lax.rem(y + (i + 4), 4)
        else:
            major, minor = lax.rem(y + (blk + 4), 4), lax.rem(z + (i + 4), 4)
        return self.c * 512 + ab * 256 + major * 64, minor * 16
    def sl(self, l, ab, i):
        a, b = self.rows(ab, i)
        return self.wq.at[l, pl.ds(pl.multiple_of(a + b, 16), 16), :]
    def slh(self, l, ab, i, h):
        a, b = self.rows(ab, i)
        return self.wq.at[l, pl.ds(pl.multiple_of(a + b, 16), 16), pl.ds(h * 1536, 1536)]
    def blk(self, l, ab, k):
        a, _ = self.rows(ab, 0, k)
        return self.wq.at[l, pl.ds(pl.multiple_of(a, 64), 64), :]
    def blkh(self, l, ab, k, h):
        a, _ = self.rows(ab, 0, k)
        return self.wq.at[l, pl.ds(pl.multiple_of(a + h * 32, 32), 32), :]
    def wop(self, l, h):
        return self.wo.at[l, pl.ds(pl.multiple_of(self.c * 512 + h * 256, 256), 256), :]
    def layer_of(self, d):
        return lax.rem(self.x + d, 4)
    def stage_layer(self, j):
        return j + (self.x <= j).astype(jnp.int32)
    def start_x(self):
        x = self.x
        for ab in (0, 1):
            a, b = self.rows(ab, 0)
            src = self.wq_in.at[0, pl.ds(pl.multiple_of(a + b, 16), 16), :]
            for dx, d in (((1, 3), (-1, 1)) if ab == 0 else ((-1, 1), (1, 3))):
                self.send(src, self.sl(x, ab, 0), self.xs.at[ab, d - 1], self.xr.at[ab, d - 1], self.dev(dx=dx))
    def wo_own(self, second):
        copies = []
        for dx, d, h in ((1, 3, second), (-1, 1, 1 - second)):
            src = self.wo_in.at[0, pl.ds(pl.multiple_of(self.c * 512 + h * 256, 256), 256), :]
            sems = self.xs.at[2 + h, d - 1], self.xr.at[2 + h, d - 1]
            copies.append(self.copy(src, self.wop(self.x, h), *sems, self.dev(dx=dx)))
        return copies

    def wo_first(self):
        for cp in self.wo_own(0):
            cp.start()
            self.pending.append(cp)
        second = self.wo_own(1)
        self.pending.extend(second)

        @pl.when(self.x == 0)
        def _():
            for cp in second:
                cp.start()

    def wo_forward(self):
        for h, d, dx in ((0, 3, 1), (1, 1, -1)):
            r = self.wop(self.layer_of(d), h)
            self.recv(r, self.xs.at[2 + h, d - 1], self.xr.at[2 + h, d - 1])
            self.send(r, r, self.xs.at[2 + h, 1], self.xr.at[2 + h, 1], self.dev(dx=dx))
            self.dd_send(r, 8 + h, d - 1)

        @pl.when(self.x != 0)
        def _():
            for cp in self.wo_own(1):
                cp.start()

    def wo_ready(self, layer):
        dist = lax.rem(layer - self.x + 4, 4)
        for d, hs in ((1, (0,)), (2, (0, 1)), (3, (1,))):
            if layer == 0:
                for h in hs:
                    r = self.wop(self.layer_of(d), h)
                    self.pending.append(
                        self.copy(r, r, self.ds.at[8 + h, d - 1], self.dr.at[8 + h, d - 1], self.dev(dc=1))
                    )

            @pl.when(dist == d)
            def _():
                for h in hs:
                    r = self.wop(self.layer_of(d), h)
                    self.recv(r, self.xs.at[2 + h, d - 1], self.xr.at[2 + h, d - 1])
                    self.copy(r, r, self.ds.at[8 + h, d - 1], self.dr.at[8 + h, d - 1], self.dev(dc=1)).start()
                g = self.other()
                for h in (0, 1):
                    self.recv(g.wop(self.layer_of(d), h), self.ds.at[8 + h, d - 1], self.dr.at[8 + h, d - 1])

    def gains_start(self, g_in, g_all):
        for dx in (1, 2, 3):
            self.send(g_in, g_all.at[self.x], self.gs.at[dx - 1], self.gr.at[dx - 1], self.dev(dx=dx))

    def gains_wait(self, g_all):
        for dx in (1, 2, 3):
            self.recv(g_all.at[self.layer_of(4 - dx)], self.gs.at[dx - 1], self.gr.at[dx - 1])

    def exchange_copy(self, k, send, land):
        src = send.at[pl.ds(pl.multiple_of(self.peer(k)[1] * 16, 16), 16), :]
        dst = land.at[pl.ds(pl.multiple_of(self.q * 16, 16), 16), :]
        return self.copy(src, dst, self.es.at[k], self.er.at[k], self.peer(k))

    def exchange_start(self, send, land):
        @pl.loop(1, 32)
        def _(k):
            self.exchange_copy(k, send, land).start()

        rows = pl.ds(pl.multiple_of(self.q * 16, 16), 16)
        pltpu.make_async_copy(send.at[rows, :], land.at[rows, :], self.es.at[0]).start()

    def exchange_wait(self, send, land):
        @pl.loop(1, 32)
        def _(k):
            rows = pl.ds(pl.multiple_of(self.source(k) * 16, 16), 16)
            self.recv(land.at[rows, :], self.es.at[k], self.er.at[k])

        rows = pl.ds(pl.multiple_of(self.q * 16, 16), 16)
        pltpu.make_async_copy(send.at[rows, :], land.at[rows, :], self.es.at[0]).wait()

    def exchange_drain(self, send, land):
        @pl.loop(1, 32)
        def _(k):
            self.exchange_copy(k, send, land).wait_send()

    def own_copies(self, frames_in, frames, g_in, g_all):
        return [
            pltpu.make_async_copy(frames_in, frames, self.own.at[0]),
            pltpu.make_async_copy(g_in, g_all.at[self.x], self.own.at[1]),
            pltpu.make_async_copy(self.wq_in.at[0], self.wq.at[self.x], self.own.at[2]),
            pltpu.make_async_copy(self.wo_in.at[0], self.wo.at[self.x], self.own.at[3]),
        ]

    def x_forward_qkv(self):
        for ab, d, dx in ((0, 3, 1), (1, 1, -1)):
            l = self.layer_of(d)
            self.recv(self.sl(l, ab, 0), self.xs.at[ab, d - 1], self.xr.at[ab, d - 1])
            self.send(self.sl(l, ab, 0), self.sl(l, ab, 0), self.xs.at[ab, 1], self.xr.at[ab, 1], self.dev(dx=dx))
    def slices_ready(self, j):
        dist = lax.rem(self.stage_layer(j) - self.x + 4, 4)
        for d, abs_ in ((1, (0,)), (2, (0, 1)), (3, (1,))):

            @pl.when(dist == d)
            def _():
                for ab in abs_:
                    self.recv(self.sl(self.layer_of(d), ab, 0), self.xs.at[ab, d - 1], self.xr.at[ab, d - 1])

    def dd_send(self, ref, a, b):
        self.send(ref, ref, self.ds.at[a, b], self.dr.at[a, b], self.dev(dc=1))

    def ax(self, phase, ab, s):
        if (phase == 1) == (ab == 0):
            return self.dev(dy=s)
        return self.dev(dz=s)
    def p1s1(self, j):
        l = self.stage_layer(j)
        for n in (0, 1):
            for k, s in enumerate((1, -1)):
                for ab in (0, 1):
                    h = k if n == 0 else 1 - k
                    r = self.slh(l, ab, 0, h)
                    self.send(r, r, self.p1s.at[ab, 2 * n + k, j], self.p1r.at[ab, 2 * n + k, j], self.ax(1, ab, s))
    def p1s2(self, j):
        l = self.stage_layer(j)
        for k, s in enumerate((1, -1)):
            for ab in (0, 1):
                r = self.slh(l, ab, -s, k)
                self.recv(r, self.p1s.at[ab, k, j], self.p1r.at[ab, k, j])
                self.send(r, r, self.p1s.at[ab, 4 + k, j], self.p1r.at[ab, 4 + k, j], self.ax(1, ab, s))
    def p2s1(self, j):
        l = self.stage_layer(j)
        for ab in (0, 1):
            for k, s in enumerate((1, -1)):
                self.recv(self.slh(l, ab, -s, 1 - k), self.p1s.at[ab, 2 + k, j], self.p1r.at[ab, 2 + k, j])
                self.recv(self.slh(l, ab, 2, k), self.p1s.at[ab, 4 + k, j], self.p1r.at[ab, 4 + k, j])
        for n in (0, 1):
            for k, s in enumerate((1, -1)):
                for ab in (0, 1):
                    h = k if n == 0 else 1 - k
                    r = self.blkh(l, ab, 0, h)
                    self.send(r, r, self.p2s.at[ab, 2 * n + k, j], self.p2r.at[ab, 2 * n + k, j], self.ax(2, ab, s))
        for ab in (0, 1):
            self.dd_send(self.blk(l, ab, 0), ab * 4, j)
    def p2s2(self, j):
        l = self.stage_layer(j)
        for k, s in enumerate((1, -1)):
            for ab in (0, 1):
                r = self.blkh(l, ab, -s, k)
                self.recv(r, self.p2s.at[ab, k, j], self.p2r.at[ab, k, j])
                self.send(r, r, self.p2s.at[ab, 4 + k, j], self.p2r.at[ab, 4 + k, j], self.ax(2, ab, s))
    def fin(self, j):
        l = self.stage_layer(j)
        for ab in (0, 1):
            for k, s in enumerate((1, -1)):
                self.recv(self.blkh(l, ab, -s, 1 - k), self.p2s.at[ab, 2 + k, j], self.p2r.at[ab, 2 + k, j])
                self.dd_send(self.blk(l, ab, -s), ab * 4 + 1 + k, j)
        for ab in (0, 1):
            for k in (0, 1):
                self.recv(self.blkh(l, ab, 2, k), self.p2s.at[ab, 4 + k, j], self.p2r.at[ab, 4 + k, j])
            self.dd_send(self.blk(l, ab, 2), ab * 4 + 3, j)
    def other(self):
        g = Gather.__new__(Gather)
        g.__dict__.update(self.__dict__)
        g.c = 1 - self.c
        return g
    def qkv_ready(self, j):
        g = self.other()
        l = self.stage_layer(j)
        for ab in (0, 1):
            for n, k in ((0, 0), (1, -1), (2, 1), (3, 2)):
                self.recv(g.blk(l, ab, k), self.ds.at[ab * 4 + n, j], self.dr.at[ab * 4 + n, j])

    def drain(self):
        for cp in self.pending:
            cp.wait_send()


def norm_into(x_ref, gain, h_ref, m):
    @pl.loop(0, m // 128)
    def _(i):
        r = pl.ds(pl.multiple_of(i * 128, 128), 128)
        v = x_ref[r, :].astype(F32)
        ms = jnp.mean(v * v, axis=-1, keepdims=True)
        h_ref[r, :] = (v * lax.rsqrt(ms + 1e-06) * gain).astype(BF)

def qkv_into(h_ref, w_ref, qkv_ref, m, tn=1024):
    @pl.loop(0, 3072 // tn)
    def _(i):
        cidx = pl.ds(pl.multiple_of(i * tn, tn), tn)
        qkv_ref[pl.ds(0, m), cidx] = jnp.dot(h_ref[pl.ds(0, m), :], w_ref[:, cidx], preferred_element_type=F32).astype(BF)

def out_into(ctx_ref, w_ref, x_ref, y_ref, m, tn=512):
    @pl.loop(0, 1024 // tn)
    def _(i):
        cidx = pl.ds(pl.multiple_of(i * tn, tn), tn)
        u = jnp.dot(ctx_ref[pl.ds(0, m), :], w_ref[:, cidx], preferred_element_type=F32)
        y_ref[pl.ds(0, m), cidx] = (x_ref[pl.ds(0, m), cidx].astype(F32) + u).astype(BF)

def attend(q2, k2, v2, mask, lo, ind):
    z = jnp.zeros((), BF)
    kk = jnp.concatenate([jnp.where(lo, k2, z), jnp.where(lo, z, k2)], axis=0)
    vv = jnp.concatenate([jnp.where(lo, v2, z), jnp.where(lo, z, v2)], axis=0)
    vv = jnp.concatenate([vv, ind], axis=1)
    s = lax.dot_general(q2, kk, (((1,), (1,)), ((), ())), preferred_element_type=F32)
    if mask is not None:
        s = jnp.where(mask, s, -1e30)
    halves = []
    for n in (0, 1):
        t = s[:, n * 128:n * 128 + 128]
        t = jnp.exp2((t - jnp.max(t, axis=-1, keepdims=True)) * 0.18033688011112042)
        halves.append(t.astype(BF))
    o = jnp.dot(jnp.concatenate(halves, axis=1), vv, preferred_element_type=F32)
    return (o[:, :128] / o[:, 128:]).astype(BF)

def attention_into(kind, qkv_ref, ctx_ref, blocks, pairs=1):
    lo = lax.broadcasted_iota(jnp.int32, (128, 128), 1) < 64
    one, z = jnp.ones((), BF), jnp.zeros((), BF)
    ind = jnp.concatenate([jnp.where(lo, one, z), jnp.where(lo, z, one)], axis=0)
    i = lax.broadcasted_iota(jnp.int32, (128, 256), 0)
    j = lax.rem(lax.broadcasted_iota(jnp.int32, (128, 256), 1), 128)
    mask = None
    if kind == "frame":
        mask = lax.rem(i, 32) == lax.rem(j, 32)
    if kind == "row":
        mask = (lax.rem(i, 8) == lax.rem(j, 8)) & (i >= j)
    @pl.loop(0, HEADS // 2 // pairs)
    def _(step):
        for p in range(pairs):
            for b in range(blocks):
                first = (step * pairs + p) * 128

                def get(base):
                    c = pl.ds(pl.multiple_of(base + first, 128), 128)
                    if kind == "frame":
                        parts = [qkv_ref[pl.ds(f * 128 + b * 32, 32), c] for f in range(4)]
                        return jnp.concatenate(parts, axis=0)
                    return qkv_ref[pl.ds(b * 128, 128), c]

                o = attend(get(0), get(1024), get(2048), mask, lo, ind)
                c = pl.ds(pl.multiple_of(first, 128), 128)
                if kind == "frame":
                    for f in range(4):
                        ctx_ref[pl.ds(f * 128 + b * 32, 32), c] = o[f * 32 : f * 32 + 32]
                else:
                    ctx_ref[pl.ds(b * 128, 128), c] = o


def select_matrix(owner_row, owner_col, pick_ref):
    before = lax.broadcasted_iota(jnp.int32, (128, 128), 0) < lax.broadcasted_iota(jnp.int32, (128, 128), 1)
    alike = (owner_col == owner_row) & before
    slot = jnp.sum(jnp.where(alike, 1.0, 0.0), axis=0, keepdims=True)
    code = owner_row.astype(F32) * 8.0 + slot
    code = jnp.concatenate([code, code], axis=1)
    k = lax.broadcasted_iota(jnp.int32, (512, 256), 0)
    r = lax.broadcasted_iota(jnp.int32, (512, 256), 1)
    want = ((k // 16) * 8 + lax.rem(k, 8)).astype(F32)
    hit = (code == want) & (lax.rem(k // 8, 2) == r // 128)
    pick_ref[...] = jnp.where(hit, 1.0, 0.0).astype(BF)


def kernel(
    order, frames_in, owner_row, owner_col, wq_in, wo_in, g_in, out,
    wq, wo, g_all, frames, clip, pick, send, vol, h, qkv, *sems
):
    g = Gather(wq_in, wo_in, wq, wo, sems)
    g.barrier()
    g.start_x()
    own = g.own_copies(frames_in, frames, g_in, g_all)
    for cp in own:
        cp.start()
    g.gains_start(g_in, g_all)
    g.x_forward_qkv()
    g.slices_ready(0)
    g.p1s1(0)
    g.slices_ready(1)
    g.p1s1(1)
    g.wo_first()
    g.p1s2(0)
    g.slices_ready(2)
    g.p1s1(2)
    g.p1s2(1)
    g.p2s1(0)
    select_matrix(owner_row[...], owner_col[...], pick)
    own[0].wait()
    turn = order[3 - g.x]
    clip[...] = frames[turn].reshape(256, 1024)
    g.p1s2(2)
    own[1].wait()
    g.gains_wait(g_all)
    norm_into(clip, g_all[0], h, 256)
    g.p2s2(0)
    g.p2s1(1)
    g.wo_forward()
    g.fin(0)
    own[2].wait()
    own[3].wait()
    g.qkv_ready(0)
    qkv_into(h, wq.at[0], qkv, 256)
    g.p2s2(1)
    attention_into("column", qkv, h, 2, 4)
    g.wo_ready(0)
    out_into(h, wo.at[0], clip, clip, 256)

    @pl.loop(0, 2)
    def _(i):
        c = pl.ds(pl.multiple_of(i * 512, 512), 512)
        send[:, c] = jnp.dot(pick[...], clip[:, c], preferred_element_type=F32).astype(BF)

    g.exchange_start(send, vol)
    g.p2s1(2)
    g.fin(1)
    g.qkv_ready(1)
    g.exchange_wait(send, vol)
    norm_into(vol, g_all[1], h, 512)
    qkv_into(h, wq.at[1], qkv, 512)
    g.p2s2(2)
    attention_into("frame", qkv, h, 4, 4)
    g.wo_ready(1)
    out_into(h, wo.at[1], vol, vol, 512)
    g.fin(2)
    g.wo_ready(2)
    g.wo_ready(3)
    g.qkv_ready(2)
    for l in (2, 3):
        norm_into(vol, g_all[l], h, 512)
        qkv_into(h, wq.at[l], qkv, 512)
        attention_into("row", qkv, h, 4, 4)
        out_into(h, wo.at[l], vol, out if l == 3 else vol, 512)
    g.exchange_drain(send, vol)
    g.drain()


def local(frames_in, order, owner, qkv_weight, out_weight, gains):
    vmem = pl.BlockSpec(memory_space=pltpu.VMEM)
    hbm = pl.BlockSpec(memory_space=pl.ANY)
    dma = pltpu.SemaphoreType.DMA
    result = pl.pallas_call(
        kernel,
        out_shape=jax.ShapeDtypeStruct((512, 1024), BF),
        in_specs=[pl.BlockSpec(memory_space=pltpu.SMEM), hbm, vmem, vmem, hbm, hbm, hbm],
        out_specs=vmem,
        scratch_shapes=[
            pltpu.VMEM((4, 1024, 3072), BF),
            pltpu.VMEM((4, 1024, 1024), BF),
            pltpu.VMEM((4, 1, 1024), F32),
            pltpu.VMEM((4, 2, 128, 1024), BF),
            pltpu.VMEM((256, 1024), BF),
            pltpu.VMEM((512, 256), BF),
            pltpu.VMEM((512, 1024), BF),
            pltpu.VMEM((512, 1024), BF),
            pltpu.VMEM((512, 1024), BF),
            pltpu.VMEM((512, 3072), BF),
            dma((4, 3)), dma((4, 3)),
            dma((2, 6, 3)), dma((2, 6, 3)),
            dma((2, 6, 3)), dma((2, 6, 3)),
            dma((10, 3)), dma((10, 3)),
            dma((3,)), dma((3,)),
            dma((32,)), dma((32,)),
            dma((4,)),
        ],
        compiler_params=pltpu.CompilerParams(
            collective_id=0, has_side_effects=True, vmem_limit_bytes=60 * 1024 * 1024
        ),
    )(order, frames_in, owner[None, :], owner[:, None], qkv_weight, out_weight, gains)
    return result.reshape(1, 64, 8, 1024)


def solution(mesh):
    placed = (
        P(None, "seq", None, None),
        P(),
        P(),
        P("section", None, None),
        P("section", None, None),
        P("section", None),
    )
    return jax.shard_map(
        local,
        mesh=mesh,
        in_specs=placed,
        out_specs=P("section", None, "seq", None),
        check_vma=False,
    )
```

```python
import functools

import jax
import jax.numpy as jnp
from jax import lax
from jax.experimental import pallas as pl
from jax.experimental.pallas import tpu as pltpu
from jax.sharding import PartitionSpec as P

MESH = pl.DeviceIdType.MESH
HEADS = 16
F32, BF = jnp.float32, jnp.bfloat16


class Lazy:
    def __init__(self, ref):
        self.ref, self.at = ref, self

    def __getitem__(self, index):
        return self.ref, index


def view(sem):
    return sem[0].at[sem[1]] if isinstance(sem, tuple) else sem


class Gather:
    def __init__(self, wq_in, wo_in, wq, wo, sems):
        self.wq_in, self.wo_in, self.wq, self.wo = wq_in, wo_in, wq, wo
        lazy = [Lazy(ref) for ref in sems[:10]]
        (self.xs, self.xr, self.p1s, self.p1r, self.p2s, self.p2r) = lazy[:6]
        (self.ds, self.dr, self.fs, self.fr) = lazy[6:]
        (self.gs, self.gr, self.es, self.er, self.own) = sems[10:]
        self.x = lax.axis_index("section")
        self.q = lax.axis_index("seq")
        self.c = lax.rem(self.q, 2)
        self.y = lax.rem(self.q // 2, 4)
        self.z = self.q // 8
        self.pending = []
        self.key = "all"
        x = self.x
        self.conds = {"x0": x == 0, "x1": x == 1, "x2": x == 2, "x3": x == 3}
        self.conds |= {"own": x != 0, "d1": x != 3, "d2": x != 2, "d3": x != 1}

    def when(self, key):
        def run(f):
            before = self.key
            self.key = key if before == "all" else before + " " + key
            pl.when(self.conds[key])(f)
            self.key = before

        return run

    def dev(self, dx=0, dy=0, dz=0, dc=0):
        x = lax.rem(self.x + (dx + 4), 4)
        y = lax.rem(self.y + (dy + 4), 4)
        z = lax.rem(self.z + (dz + 4), 4)
        c = lax.rem(self.c + dc, 2)
        return (x, (z * 4 + y) * 2 + c)
    def peer(self, k):
        return self.dev(0, lax.rem(k // 2, 4), k // 8, lax.rem(k, 2))

    def source(self, k):
        return self.dev(0, 4 - lax.rem(k // 2, 4), 4 - k // 8, 2 - lax.rem(k, 2))[1]

    def barrier(self):
        sem = pltpu.get_barrier_semaphore()
        for dx in (1, 2, 3):
            pl.semaphore_signal(sem, inc=1, device_id=self.dev(dx=dx), device_id_type=MESH)

        @pl.loop(1, 32)
        def _(k):
            pl.semaphore_signal(sem, inc=1, device_id=self.peer(k), device_id_type=MESH)

        pl.semaphore_wait(sem, 34)

    def copy(self, src, dst, ss, rs, dev):
        return pltpu.make_async_remote_copy(
            src_ref=src, dst_ref=dst, send_sem=view(ss), recv_sem=view(rs), device_id=dev, device_id_type=MESH
        )

    def send(self, src, dst, ss, rs, dev):
        self.copy(src, dst, ss, rs, dev).start()
        self.sent(src.shape, ss)

    def sent(self, shape, ss, key=None):
        self.pending.append((key or self.key, shape, ss))

    def recv(self, dst, ss, rs):
        self.copy(dst, dst, ss, rs, self.dev(dc=1)).wait_recv()
    def rows(self, ab, i=0, blk=0):
        y, z = self.y, self.z
        if ab == 0:
            major, minor = lax.rem(z + (blk + 4), 4), lax.rem(y + (i + 4), 4)
        else:
            major, minor = lax.rem(y + (blk + 4), 4), lax.rem(z + (i + 4), 4)
        return self.c * 512 + ab * 256 + major * 64, minor * 16
    def sl(self, l, ab, i):
        a, b = self.rows(ab, i)
        return self.wq.at[l, pl.ds(pl.multiple_of(a + b, 16), 16), :]
    def slh(self, l, ab, i, h):
        a, b = self.rows(ab, i)
        return self.wq.at[l, pl.ds(pl.multiple_of(a + b, 16), 16), pl.ds(h * 1536, 1536)]
    def blk(self, l, ab, k):
        a, _ = self.rows(ab, 0, k)
        return self.wq.at[l, pl.ds(pl.multiple_of(a, 64), 64), :]
    def blkh(self, l, ab, k, h):
        a, _ = self.rows(ab, 0, k)
        return self.wq.at[l, pl.ds(pl.multiple_of(a + h * 32, 32), 32), :]
    def wop(self, l, h):
        return self.wo.at[l, pl.ds(pl.multiple_of(self.c * 512 + h * 256, 256), 256), :]
    def layer_of(self, d):
        return lax.rem(self.x + d, 4)
    def stage_layer(self, j):
        return j + 1 + ((self.x > 0) & (self.x <= j + 1)).astype(jnp.int32)
    def start_x(self):
        @self.when("own")
        def _():
            for ab in (0, 1):
                a, b = self.rows(ab, 0)
                src = self.wq_in.at[0, pl.ds(pl.multiple_of(a + b, 16), 16), :]
                for dx, d in ((1, 3), (-1, 1)) if ab == 0 else ((-1, 1), (1, 3)):
                    sems = self.xs.at[ab, d - 1], self.xr.at[ab, d - 1]
                    self.send(src, self.sl(self.x, ab, 0), *sems, self.dev(dx=dx))

    def wo_own(self, second):
        @self.when("own")
        def _():
            for dx, d, h in ((1, 3, second), (-1, 1, 1 - second)):
                src = self.wo_in.at[0, pl.ds(pl.multiple_of(self.c * 512 + h * 256, 256), 256), :]
                sems = self.xs.at[2 + h, d - 1], self.xr.at[2 + h, d - 1]
                self.send(src, self.wop(self.x, h), *sems, self.dev(dx=dx))

    def wo_forward(self):
        for h, d, dx in ((0, 3, 1), (1, 1, -1)):

            @self.when(f"d{d}")
            def _():
                r = self.wop(self.layer_of(d), h)
                self.recv(r, self.xs.at[2 + h, d - 1], self.xr.at[2 + h, d - 1])
                self.send(r, r, self.xs.at[2 + h, 1], self.xr.at[2 + h, 1], self.dev(dx=dx))
                self.dd_send(r, 8 + h, d - 1)

    def wo_ready(self, layer):
        dist = lax.rem(layer - self.x + 4, 4)
        for d, hs in ((1, (0,)), (2, (0, 1)), (3, (1,))):
            if layer == 1:
                for h in hs:
                    self.sent((256, 1024), self.ds.at[8 + h, d - 1], f"d{d}")

            @pl.when(dist == d)
            def _():
                for h in hs:
                    r = self.wop(self.layer_of(d), h)
                    self.recv(r, self.xs.at[2 + h, d - 1], self.xr.at[2 + h, d - 1])
                    self.copy(r, r, self.ds.at[8 + h, d - 1], self.dr.at[8 + h, d - 1], self.dev(dc=1)).start()
                g = self.other()
                for h in (0, 1):
                    self.recv(g.wop(self.layer_of(d), h), self.ds.at[8 + h, d - 1], self.dr.at[8 + h, d - 1])

    def gains_copies(self, g_in, g_all):
        dst = g_all.at[self.x]
        return [
            self.copy(g_in, dst, self.gs.at[dx - 1], self.gr.at[dx - 1], self.dev(dx=dx)) for dx in (1, 2, 3)
        ]

    def gains_wait(self, g_all):
        for dx in (1, 2, 3):
            self.recv(g_all.at[self.layer_of(4 - dx)], self.gs.at[dx - 1], self.gr.at[dx - 1])

    def columns_send(self, x1, t):
        if t == 2:
            for n, dx in ((0, 1), (1, -1)):
                r = x1.at[2, pl.ds(n * 128, 128), :]
                self.send(r, r, self.fs.at[2 + n], self.fr.at[2 + n], self.dev(dx=dx))
        else:
            n, dx = (0, 1) if t == 1 else (1, -1)
            self.send(x1.at[t], x1.at[t], self.fs.at[n], self.fr.at[n], self.dev(dx=dx))

    def columns_relay(self, x1):
        for n, dx, key in ((0, 1, "x1"), (1, -1, "x3")):

            @self.when(key)
            def _():
                r = x1.at[2, pl.ds(n * 128, 128), :]
                self.recv(r, self.fs.at[2 + n], self.fr.at[2 + n])
                self.send(r, r, self.fs.at[4 + n], self.fr.at[4 + n], self.dev(dx=dx))

    def columns_wait(self, x1):
        for n, key, t in ((0, "x1", 1), (1, "x3", 3)):

            @self.when(key)
            def _():
                self.recv(x1.at[t], self.fs.at[n], self.fr.at[n])

        @self.when("x2")
        def _():
            for n in (0, 1):
                self.recv(x1.at[2, pl.ds(n * 128, 128), :], self.fs.at[4 + n], self.fr.at[4 + n])

    def exchange_copy(self, k, send, land):
        src = send.at[pl.ds(pl.multiple_of(self.peer(k)[1] * 16, 16), 16), :]
        dst = land.at[pl.ds(pl.multiple_of(self.q * 16, 16), 16), :]
        return self.copy(src, dst, self.es.at[k], self.er.at[k], self.peer(k))

    def exchange_start(self, send, land):
        @pl.loop(1, 32)
        def _(k):
            self.exchange_copy(k, send, land).start()

        rows = pl.ds(pl.multiple_of(self.q * 16, 16), 16)
        pltpu.make_async_copy(send.at[rows, :], land.at[rows, :], self.es.at[0]).start()

    def exchange_wait(self, send, land):
        @pl.loop(1, 32)
        def _(k):
            rows = pl.ds(pl.multiple_of(self.source(k) * 16, 16), 16)
            self.recv(land.at[rows, :], self.es.at[k], self.er.at[k])

        rows = pl.ds(pl.multiple_of(self.q * 16, 16), 16)
        pltpu.make_async_copy(send.at[rows, :], land.at[rows, :], self.es.at[0]).wait()

    def exchange_drain(self, send, land):
        @pl.loop(1, 32)
        def _(k):
            self.exchange_copy(k, send, land).wait_send()

    def own_copies(self, frames_in, frames, g_in, g_all):
        return [
            pltpu.make_async_copy(frames_in, frames, self.own.at[0]),
            pltpu.make_async_copy(g_in, g_all.at[self.x], self.own.at[1]),
            pltpu.make_async_copy(self.wq_in.at[0], self.wq.at[self.x], self.own.at[2]),
            pltpu.make_async_copy(self.wo_in.at[0], self.wo.at[self.x], self.own.at[3]),
        ]

    def x_forward_qkv(self):
        for ab, d, dx in ((0, 3, 1), (1, 1, -1)):

            @self.when(f"d{d}")
            def _():
                r = self.sl(self.layer_of(d), ab, 0)
                self.recv(r, self.xs.at[ab, d - 1], self.xr.at[ab, d - 1])
                self.send(r, r, self.xs.at[ab, 1], self.xr.at[ab, 1], self.dev(dx=dx))

    def slices_ready(self, j):
        dist = lax.rem(self.stage_layer(j) - self.x + 4, 4)
        for d, abs_ in ((1, (0,)), (2, (0, 1)), (3, (1,))):

            @pl.when(dist == d)
            def _():
                for ab in abs_:
                    self.recv(self.sl(self.layer_of(d), ab, 0), self.xs.at[ab, d - 1], self.xr.at[ab, d - 1])

    def dd_send(self, ref, a, b):
        self.send(ref, ref, self.ds.at[a, b], self.dr.at[a, b], self.dev(dc=1))

    def ax(self, phase, ab, s):
        if (phase == 1) == (ab == 0):
            return self.dev(dy=s)
        return self.dev(dz=s)
    def p1s1(self, j):
        l = self.stage_layer(j)
        for n in (0, 1):
            for k, s in enumerate((1, -1)):
                for ab in (0, 1):
                    h = k if n == 0 else 1 - k
                    r = self.slh(l, ab, 0, h)
                    self.send(r, r, self.p1s.at[ab, 2 * n + k, j], self.p1r.at[ab, 2 * n + k, j], self.ax(1, ab, s))
    def p1s2(self, j):
        l = self.stage_layer(j)
        for k, s in enumerate((1, -1)):
            for ab in (0, 1):
                r = self.slh(l, ab, -s, k)
                self.recv(r, self.p1s.at[ab, k, j], self.p1r.at[ab, k, j])
                self.send(r, r, self.p1s.at[ab, 4 + k, j], self.p1r.at[ab, 4 + k, j], self.ax(1, ab, s))
    def p2s1(self, j):
        l = self.stage_layer(j)
        for ab in (0, 1):
            for k, s in enumerate((1, -1)):
                self.recv(self.slh(l, ab, -s, 1 - k), self.p1s.at[ab, 2 + k, j], self.p1r.at[ab, 2 + k, j])
                self.recv(self.slh(l, ab, 2, k), self.p1s.at[ab, 4 + k, j], self.p1r.at[ab, 4 + k, j])
        for n in (0, 1):
            for k, s in enumerate((1, -1)):
                for ab in (0, 1):
                    h = k if n == 0 else 1 - k
                    r = self.blkh(l, ab, 0, h)
                    self.send(r, r, self.p2s.at[ab, 2 * n + k, j], self.p2r.at[ab, 2 * n + k, j], self.ax(2, ab, s))
        for ab in (0, 1):
            self.dd_send(self.blk(l, ab, 0), ab * 4, j)
    def p2s2(self, j):
        l = self.stage_layer(j)
        for k, s in enumerate((1, -1)):
            for ab in (0, 1):
                r = self.blkh(l, ab, -s, k)
                self.recv(r, self.p2s.at[ab, k, j], self.p2r.at[ab, k, j])
                self.send(r, r, self.p2s.at[ab, 4 + k, j], self.p2r.at[ab, 4 + k, j], self.ax(2, ab, s))
    def fin(self, j):
        l = self.stage_layer(j)
        for ab in (0, 1):
            for k, s in enumerate((1, -1)):
                self.recv(self.blkh(l, ab, -s, 1 - k), self.p2s.at[ab, 2 + k, j], self.p2r.at[ab, 2 + k, j])
                self.dd_send(self.blk(l, ab, -s), ab * 4 + 1 + k, j)
        for ab in (0, 1):
            for k in (0, 1):
                self.recv(self.blkh(l, ab, 2, k), self.p2s.at[ab, 4 + k, j], self.p2r.at[ab, 4 + k, j])
            self.dd_send(self.blk(l, ab, 2), ab * 4 + 3, j)
    def other(self):
        g = Gather.__new__(Gather)
        g.__dict__.update(self.__dict__)
        g.c = 1 - self.c
        return g
    def qkv_ready(self, j):
        g = self.other()
        l = self.stage_layer(j)
        for ab in (0, 1):
            for n, k in ((0, 0), (1, -1), (2, 1), (3, 2)):
                self.recv(g.blk(l, ab, k), self.ds.at[ab * 4 + n, j], self.dr.at[ab * 4 + n, j])

    def drain(self):
        def wait(items):
            for shape, ss in items:
                r = self.wq.at[0, pl.ds(0, shape[0]), pl.ds(0, shape[1])]
                self.copy(r, r, ss, self.dr.at[0, 0], self.dev(dc=1)).wait_send()

        for key in dict.fromkeys(k for k, _, _ in self.pending):
            items = [(shape, ss) for k, shape, ss in self.pending if k == key]
            if key == "all":
                wait(items)
            else:
                met = functools.reduce(jnp.logical_and, [self.conds[k] for k in key.split()])
                pl.when(met)(functools.partial(wait, items))


def norm_into(x_ref, gain, h_ref, m):
    @pl.loop(0, m // 128)
    def _(i):
        r = pl.ds(pl.multiple_of(i * 128, 128), 128)
        v = x_ref[r, :].astype(F32)
        ms = jnp.mean(v * v, axis=-1, keepdims=True)
        h_ref[r, :] = (v * lax.rsqrt(ms + 1e-06) * gain).astype(BF)

def qkv_into(h_ref, w_ref, qkv_ref, m, tn=1024):
    @pl.loop(0, 3072 // tn)
    def _(i):
        cidx = pl.ds(pl.multiple_of(i * tn, tn), tn)
        qkv_ref[pl.ds(0, m), cidx] = jnp.dot(h_ref[pl.ds(0, m), :], w_ref[:, cidx], preferred_element_type=F32).astype(BF)

def out_into(ctx_ref, w_ref, x_ref, y_ref, m, tn=512):
    @pl.loop(0, 1024 // tn)
    def _(i):
        cidx = pl.ds(pl.multiple_of(i * tn, tn), tn)
        u = jnp.dot(ctx_ref[pl.ds(0, m), :], w_ref[:, cidx], preferred_element_type=F32)
        y_ref[pl.ds(0, m), cidx] = (x_ref[pl.ds(0, m), cidx].astype(F32) + u).astype(BF)

def attend(q2, k2, v2, mask, lo, ind):
    z = jnp.zeros((), BF)
    kk = jnp.concatenate([jnp.where(lo, k2, z), jnp.where(lo, z, k2)], axis=0)
    vv = jnp.concatenate([jnp.where(lo, v2, z), jnp.where(lo, z, v2)], axis=0)
    vv = jnp.concatenate([vv, ind], axis=1)
    s = lax.dot_general(q2, kk, (((1,), (1,)), ((), ())), preferred_element_type=F32)
    if mask is not None:
        s = jnp.where(mask, s, -1e30)
    halves = []
    for n in (0, 1):
        t = s[:, n * 128:n * 128 + 128]
        t = jnp.exp2((t - jnp.max(t, axis=-1, keepdims=True)) * 0.18033688011112042)
        halves.append(t.astype(BF))
    o = jnp.dot(jnp.concatenate(halves, axis=1), vv, preferred_element_type=F32)
    return (o[:, :128] / o[:, 128:]).astype(BF)

def attention_into(kind, qkv_ref, ctx_ref, blocks, pairs=1):
    lo = lax.broadcasted_iota(jnp.int32, (128, 128), 1) < 64
    one, z = jnp.ones((), BF), jnp.zeros((), BF)
    ind = jnp.concatenate([jnp.where(lo, one, z), jnp.where(lo, z, one)], axis=0)
    i = lax.broadcasted_iota(jnp.int32, (128, 256), 0)
    j = lax.rem(lax.broadcasted_iota(jnp.int32, (128, 256), 1), 128)
    mask = None
    if kind == "frame":
        mask = lax.rem(i, 32) == lax.rem(j, 32)
    if kind == "row":
        mask = (lax.rem(i, 8) == lax.rem(j, 8)) & (i >= j)
    @pl.loop(0, HEADS // 2 // pairs)
    def _(step):
        for p in range(pairs):
            for b in range(blocks):
                first = (step * pairs + p) * 128

                def get(base):
                    c = pl.ds(pl.multiple_of(base + first, 128), 128)
                    if kind == "frame":
                        parts = [qkv_ref[pl.ds(f * 128 + b * 32, 32), c] for f in range(4)]
                        return jnp.concatenate(parts, axis=0)
                    return qkv_ref[pl.ds(b * 128, 128), c]

                o = attend(get(0), get(1024), get(2048), mask, lo, ind)
                c = pl.ds(pl.multiple_of(first, 128), 128)
                if kind == "frame":
                    for f in range(4):
                        ctx_ref[pl.ds(f * 128 + b * 32, 32), c] = o[f * 32 : f * 32 + 32]
                else:
                    ctx_ref[pl.ds(b * 128, 128), c] = o


def select_matrix(owner_row, owner_col, pick_ref):
    before = lax.broadcasted_iota(jnp.int32, (128, 128), 0) < lax.broadcasted_iota(jnp.int32, (128, 128), 1)
    alike = (owner_col == owner_row) & before
    slot = jnp.sum(jnp.where(alike, 1.0, 0.0), axis=0, keepdims=True)
    code = owner_row.astype(F32) * 8.0 + slot
    code = jnp.concatenate([code, code], axis=1)
    k = lax.broadcasted_iota(jnp.int32, (512, 256), 0)
    r = lax.broadcasted_iota(jnp.int32, (512, 256), 1)
    want = ((k // 16) * 8 + lax.rem(k, 8)).astype(F32)
    hit = (code == want) & (lax.rem(k // 8, 2) == r // 128)
    pick_ref[...] = jnp.where(hit, 1.0, 0.0).astype(BF)


def kernel(
    order, frames_in, owner_row, owner_col, wq_in, wo_in, g_in, out,
    wq, wo, g_all, frames, x1, pick, send, vol, h, qkv, *sems
):
    g = Gather(wq_in, wo_in, wq, wo, sems)

    def columns_first(t):
        x1[t] = frames[order[3 - t]].reshape(256, 1024)
        norm_into(x1.at[t], g_all[0], h, 256)
        qkv_into(h, wq.at[0], qkv, 256)

    def columns_rest(t):
        attention_into("column", qkv, h, 2, 4)
        out_into(h, wo.at[0], x1.at[t], x1.at[t], 256)

    def exchange_start():
        @pl.loop(0, 2)
        def _(i):
            c = pl.ds(pl.multiple_of(i * 512, 512), 512)
            send[:, c] = jnp.dot(pick[...], x1[g.x, :, c], preferred_element_type=F32).astype(BF)

        g.exchange_start(send, vol)

    def at0(*steps):
        @g.when("x0")
        def _():
            for step in steps:
                step()

    part = functools.partial
    g.barrier()
    g.start_x()
    own = g.own_copies(frames_in, frames, g_in, g_all)
    for cp in own:
        cp.start()
    gains = g.gains_copies(g_in, g_all)
    for cp in gains:
        cp.start()
    select_matrix(owner_row[...], owner_col[...], pick)
    for cp in own:
        cp.wait()

    def send_columns(t):
        columns_rest(t)
        g.columns_send(x1, t)

    at0(
        part(columns_first, 2),
        g.x_forward_qkv,
        part(g.slices_ready, 0),
        part(g.p1s1, 0),
        part(send_columns, 2),
        part(g.slices_ready, 1),
        part(g.p1s1, 1),
        part(g.p1s2, 0),
        part(columns_first, 3),
        part(g.slices_ready, 2),
        part(g.p1s1, 2),
        part(g.p1s2, 1),
        part(send_columns, 3),
        part(g.p2s1, 0),
        part(columns_first, 1),
        part(g.p1s2, 2),
        part(send_columns, 1),
        part(g.p2s1, 1),
        part(columns_first, 0),
        part(g.p2s2, 0),
        part(columns_rest, 0),
        exchange_start,
        g.wo_forward,
        part(g.fin, 0),
        part(g.p2s2, 1),
        part(g.p2s1, 2),
    )

    @g.when("own")
    def _():
        g.x_forward_qkv()
        g.slices_ready(0)
        g.p1s1(0)
        g.slices_ready(1)
        g.p1s1(1)
        g.wo_own(0)
        g.p1s2(0)
        g.p1s2(1)
        g.p2s1(0)
        g.columns_relay(x1)
        g.p2s2(0)
        g.wo_forward()
        g.wo_own(1)
        g.columns_wait(x1)
        exchange_start()
        g.p2s1(1)
        g.fin(0)

    def own_do(step, j):
        g.when("own")(part(step, j))

    g.gains_wait(g_all)
    g.exchange_wait(send, vol)
    norm_into(vol, g_all[1], h, 512)
    g.qkv_ready(0)
    qkv_into(h, wq.at[1], qkv, 512)
    own_do(g.p2s2, 1)
    at0(part(g.fin, 1))
    attention_into("frame", qkv, h, 4, 4)
    at0(part(g.p2s2, 2))
    g.wo_ready(1)
    out_into(h, wo.at[1], vol, vol, 512)
    own_do(g.fin, 1)
    norm_into(vol, g_all[2], h, 512)
    g.qkv_ready(1)
    qkv_into(h, wq.at[2], qkv, 512)
    attention_into("row", qkv, h, 4, 4)
    g.wo_ready(2)
    out_into(h, wo.at[2], vol, vol, 512)
    at0(part(g.fin, 2))
    norm_into(vol, g_all[3], h, 512)
    at0(part(g.qkv_ready, 2))
    g.wo_ready(3)
    qkv_into(h, wq.at[3], qkv, 512)
    attention_into("row", qkv, h, 4, 4)
    out_into(h, wo.at[3], vol, out, 512)
    for cp in gains:
        cp.wait_send()
    g.exchange_drain(send, vol)
    g.drain()


def local(frames_in, order, owner, qkv_weight, out_weight, gains):
    vmem = pl.BlockSpec(memory_space=pltpu.VMEM)
    hbm = pl.BlockSpec(memory_space=pl.ANY)
    dma = pltpu.SemaphoreType.DMA
    result = pl.pallas_call(
        kernel,
        out_shape=jax.ShapeDtypeStruct((512, 1024), BF),
        in_specs=[pl.BlockSpec(memory_space=pltpu.SMEM), hbm, vmem, vmem, hbm, hbm, hbm],
        out_specs=vmem,
        scratch_shapes=[
            pltpu.VMEM((4, 1024, 3072), BF),
            pltpu.VMEM((4, 1024, 1024), BF),
            pltpu.VMEM((4, 1, 1024), F32),
            pltpu.VMEM((4, 2, 128, 1024), BF),
            pltpu.VMEM((4, 256, 1024), BF),
            pltpu.VMEM((512, 256), BF),
            pltpu.VMEM((512, 1024), BF),
            pltpu.VMEM((512, 1024), BF),
            pltpu.VMEM((512, 1024), BF),
            pltpu.VMEM((512, 3072), BF),
            dma((4, 3)), dma((4, 3)),
            dma((2, 6, 3)), dma((2, 6, 3)),
            dma((2, 6, 3)), dma((2, 6, 3)),
            dma((10, 3)), dma((10, 3)),
            dma((6,)), dma((6,)),
            dma((3,)), dma((3,)),
            dma((32,)), dma((32,)),
            dma((4,)),
        ],
        compiler_params=pltpu.CompilerParams(
            collective_id=0, has_side_effects=True, vmem_limit_bytes=60 * 1024 * 1024
        ),
    )(order, frames_in, owner[None, :], owner[:, None], qkv_weight, out_weight, gains)
    return result.reshape(1, 64, 8, 1024)


def solution(mesh):
    placed = (
        P(None, "seq", None, None),
        P(),
        P(),
        P("section", None, None),
        P("section", None, None),
        P("section", None),
    )
    return jax.shard_map(
        local,
        mesh=mesh,
        in_specs=placed,
        out_specs=P("section", None, "seq", None),
        check_vma=False,
    )
```

```python
import functools

import jax
import jax.numpy as jnp
from jax import lax
from jax.experimental import pallas as pl
from jax.experimental.pallas import tpu as pltpu
from jax.sharding import PartitionSpec as P

MESH = pl.DeviceIdType.MESH
HEADS = 16
F32, BF = jnp.float32, jnp.bfloat16


class Lazy:
    def __init__(self, ref):
        self.ref, self.at = ref, self

    def __getitem__(self, index):
        return self.ref, index


def view(sem):
    return sem[0].at[sem[1]] if isinstance(sem, tuple) else sem


class Gather:
    def __init__(self, wq_in, wo_in, wq, wo, sems):
        self.wq_in, self.wo_in, self.wq, self.wo = wq_in, wo_in, wq, wo
        lazy = [Lazy(ref) for ref in sems[:10]]
        (self.xs, self.xr, self.p1s, self.p1r, self.p2s, self.p2r) = lazy[:6]
        (self.ds, self.dr, self.fs, self.fr) = lazy[6:]
        (self.gs, self.gr, self.es, self.er, self.own) = sems[10:]
        self.x = lax.axis_index("section")
        self.q = lax.axis_index("seq")
        self.c = lax.rem(self.q, 2)
        self.y = lax.rem(self.q // 2, 4)
        self.z = self.q // 8
        self.pending = []
        self.key = "all"
        x = self.x
        self.conds = {"x0": x == 0, "x1": x == 1, "x2": x == 2, "x3": x == 3}
        self.conds |= {"own": x != 0, "d1": x != 3, "d2": x != 2, "d3": x != 1}

    def when(self, key):
        def run(f):
            before = self.key
            self.key = key if before == "all" else before + " " + key
            pl.when(self.conds[key])(f)
            self.key = before

        return run

    def dev(self, dx=0, dy=0, dz=0, dc=0):
        x = lax.rem(self.x + (dx + 4), 4)
        y = lax.rem(self.y + (dy + 4), 4)
        z = lax.rem(self.z + (dz + 4), 4)
        c = lax.rem(self.c + dc, 2)
        return (x, (z * 4 + y) * 2 + c)
    def peer(self, k):
        return self.dev(0, lax.rem(k // 2, 4), k // 8, lax.rem(k, 2))

    def source(self, k):
        return self.dev(0, 4 - lax.rem(k // 2, 4), 4 - k // 8, 2 - lax.rem(k, 2))[1]

    def greet(self):
        sem = pltpu.get_barrier_semaphore()
        for dx in (1, 2, 3):
            pl.semaphore_signal(sem, inc=1, device_id=self.dev(dx=dx), device_id_type=MESH)

        @pl.loop(1, 32)
        def _(k):
            pl.semaphore_signal(sem, inc=1, device_id=self.peer(k), device_id_type=MESH)

    def greeted(self):
        pl.semaphore_wait(pltpu.get_barrier_semaphore(), 34)

    def copy(self, src, dst, ss, rs, dev):
        return pltpu.make_async_remote_copy(
            src_ref=src, dst_ref=dst, send_sem=view(ss), recv_sem=view(rs), device_id=dev, device_id_type=MESH
        )

    def send(self, src, dst, ss, rs, dev):
        self.copy(src, dst, ss, rs, dev).start()
        self.sent(src.shape, ss)

    def sent(self, shape, ss, key=None):
        self.pending.append((key or self.key, shape, ss))

    def recv(self, dst, ss, rs):
        self.copy(dst, dst, ss, rs, self.dev(dc=1)).wait_recv()
    def rows(self, ab, i=0, blk=0):
        y, z = self.y, self.z
        if ab == 0:
            major, minor = lax.rem(z + (blk + 4), 4), lax.rem(y + (i + 4), 4)
        else:
            major, minor = lax.rem(y + (blk + 4), 4), lax.rem(z + (i + 4), 4)
        return self.c * 512 + ab * 256 + major * 64, minor * 16
    def sl(self, l, ab, i):
        a, b = self.rows(ab, i)
        return self.wq.at[l, pl.ds(pl.multiple_of(a + b, 16), 16), :]
    def slh(self, l, ab, i, h):
        a, b = self.rows(ab, i)
        return self.wq.at[l, pl.ds(pl.multiple_of(a + b, 16), 16), pl.ds(h * 1536, 1536)]
    def blk(self, l, ab, k):
        a, _ = self.rows(ab, 0, k)
        return self.wq.at[l, pl.ds(pl.multiple_of(a, 64), 64), :]
    def blkh(self, l, ab, k, h):
        a, _ = self.rows(ab, 0, k)
        return self.wq.at[l, pl.ds(pl.multiple_of(a + h * 32, 32), 32), :]
    def wop(self, l, h):
        return self.wo.at[l, pl.ds(pl.multiple_of(self.c * 512 + h * 256, 256), 256), :]
    def layer_of(self, d):
        return lax.rem(self.x + d, 4)
    def stage_layer(self, j):
        return j + 1 + ((self.x > 0) & (self.x <= j + 1)).astype(jnp.int32)
    def start_x(self):
        @self.when("own")
        def _():
            for ab in (0, 1):
                a, b = self.rows(ab, 0)
                src = self.wq_in.at[0, pl.ds(pl.multiple_of(a + b, 16), 16), :]
                for dx, d in ((1, 3), (-1, 1)) if ab == 0 else ((-1, 1), (1, 3)):
                    sems = self.xs.at[ab, d - 1], self.xr.at[ab, d - 1]
                    self.send(src, self.sl(self.x, ab, 0), *sems, self.dev(dx=dx))

    def wo_own(self, second):
        @self.when("own")
        def _():
            for dx, d, h in ((1, 3, second), (-1, 1, 1 - second)):
                src = self.wo_in.at[0, pl.ds(pl.multiple_of(self.c * 512 + h * 256, 256), 256), :]
                sems = self.xs.at[2 + h, d - 1], self.xr.at[2 + h, d - 1]
                self.send(src, self.wop(self.x, h), *sems, self.dev(dx=dx))

    def wo_forward(self):
        for h, d, dx in ((0, 3, 1), (1, 1, -1)):

            @self.when(f"d{d}")
            def _():
                r = self.wop(self.layer_of(d), h)
                self.recv(r, self.xs.at[2 + h, d - 1], self.xr.at[2 + h, d - 1])
                self.send(r, r, self.xs.at[2 + h, 1], self.xr.at[2 + h, 1], self.dev(dx=dx))
                self.dd_send(r, 8 + h, d - 1)

    def wo_ready(self, layer):
        dist = lax.rem(layer - self.x + 4, 4)
        for d, hs in ((1, (0,)), (2, (0, 1)), (3, (1,))):
            if layer == 1:
                for h in hs:
                    self.sent((256, 1024), self.ds.at[8 + h, d - 1], f"d{d}")

            @pl.when(dist == d)
            def _():
                for h in hs:
                    r = self.wop(self.layer_of(d), h)
                    self.recv(r, self.xs.at[2 + h, d - 1], self.xr.at[2 + h, d - 1])
                    self.copy(r, r, self.ds.at[8 + h, d - 1], self.dr.at[8 + h, d - 1], self.dev(dc=1)).start()
                g = self.other()
                for h in (0, 1):
                    self.recv(g.wop(self.layer_of(d), h), self.ds.at[8 + h, d - 1], self.dr.at[8 + h, d - 1])

    def gains_copies(self, g_in, g_all):
        dst = g_all.at[self.x]
        return [
            self.copy(g_in, dst, self.gs.at[dx - 1], self.gr.at[dx - 1], self.dev(dx=dx)) for dx in (1, 2, 3)
        ]

    def gains_wait(self, g_all):
        for dx in (1, 2, 3):
            self.recv(g_all.at[self.layer_of(4 - dx)], self.gs.at[dx - 1], self.gr.at[dx - 1])

    def columns_send(self, x1, t):
        if t == 2:
            for n, dx in ((0, 1), (1, -1)):
                r = x1.at[2, pl.ds(n * 128, 128), :]
                self.send(r, r, self.fs.at[2 + n], self.fr.at[2 + n], self.dev(dx=dx))
        else:
            n, dx = (0, 1) if t == 1 else (1, -1)
            self.send(x1.at[t], x1.at[t], self.fs.at[n], self.fr.at[n], self.dev(dx=dx))

    def columns_relay(self, x1):
        for n, dx, key in ((0, 1, "x1"), (1, -1, "x3")):

            @self.when(key)
            def _():
                r = x1.at[2, pl.ds(n * 128, 128), :]
                self.recv(r, self.fs.at[2 + n], self.fr.at[2 + n])
                self.send(r, r, self.fs.at[4 + n], self.fr.at[4 + n], self.dev(dx=dx))

    def columns_wait(self, x1):
        for n, key, t in ((0, "x1", 1), (1, "x3", 3)):

            @self.when(key)
            def _():
                self.recv(x1.at[t], self.fs.at[n], self.fr.at[n])

        @self.when("x2")
        def _():
            for n in (0, 1):
                self.recv(x1.at[2, pl.ds(n * 128, 128), :], self.fs.at[4 + n], self.fr.at[4 + n])

    def exchange_copy(self, k, send, land):
        src = send.at[pl.ds(pl.multiple_of(self.peer(k)[1] * 16, 16), 16), :]
        dst = land.at[pl.ds(pl.multiple_of(self.q * 16, 16), 16), :]
        return self.copy(src, dst, self.es.at[k], self.er.at[k], self.peer(k))

    def exchange_start(self, send, land):
        @pl.loop(1, 32)
        def _(k):
            self.exchange_copy(k, send, land).start()

        rows = pl.ds(pl.multiple_of(self.q * 16, 16), 16)
        pltpu.make_async_copy(send.at[rows, :], land.at[rows, :], self.es.at[0]).start()

    def exchange_wait(self, send, land):
        @pl.loop(1, 32)
        def _(k):
            rows = pl.ds(pl.multiple_of(self.source(k) * 16, 16), 16)
            self.recv(land.at[rows, :], self.es.at[k], self.er.at[k])

        rows = pl.ds(pl.multiple_of(self.q * 16, 16), 16)
        pltpu.make_async_copy(send.at[rows, :], land.at[rows, :], self.es.at[0]).wait()

    def exchange_drain(self, send, land):
        @pl.loop(1, 32)
        def _(k):
            self.exchange_copy(k, send, land).wait_send()

    def own_copies(self, frames_in, frames, g_in, g_all):
        return [
            pltpu.make_async_copy(frames_in, frames, self.own.at[0]),
            pltpu.make_async_copy(g_in, g_all.at[self.x], self.own.at[1]),
            pltpu.make_async_copy(self.wq_in.at[0], self.wq.at[self.x], self.own.at[2]),
            pltpu.make_async_copy(self.wo_in.at[0], self.wo.at[self.x], self.own.at[3]),
        ]

    def x_forward_qkv(self):
        for ab, d, dx in ((0, 3, 1), (1, 1, -1)):

            @self.when(f"d{d}")
            def _():
                r = self.sl(self.layer_of(d), ab, 0)
                self.recv(r, self.xs.at[ab, d - 1], self.xr.at[ab, d - 1])
                self.send(r, r, self.xs.at[ab, 1], self.xr.at[ab, 1], self.dev(dx=dx))

    def slices_ready(self, j):
        dist = lax.rem(self.stage_layer(j) - self.x + 4, 4)
        for d, abs_ in ((1, (0,)), (2, (0, 1)), (3, (1,))):

            @pl.when(dist == d)
            def _():
                for ab in abs_:
                    self.recv(self.sl(self.layer_of(d), ab, 0), self.xs.at[ab, d - 1], self.xr.at[ab, d - 1])

    def dd_send(self, ref, a, b):
        self.send(ref, ref, self.ds.at[a, b], self.dr.at[a, b], self.dev(dc=1))

    def ax(self, phase, ab, s):
        if (phase == 1) == (ab == 0):
            return self.dev(dy=s)
        return self.dev(dz=s)
    def p1s1(self, j):
        l = self.stage_layer(j)
        for n in (0, 1):
            for k, s in enumerate((1, -1)):
                for ab in (0, 1):
                    h = k if n == 0 else 1 - k
                    r = self.slh(l, ab, 0, h)
                    self.send(r, r, self.p1s.at[ab, 2 * n + k, j], self.p1r.at[ab, 2 * n + k, j], self.ax(1, ab, s))
    def p1s2(self, j):
        l = self.stage_layer(j)
        for k, s in enumerate((1, -1)):
            for ab in (0, 1):
                r = self.slh(l, ab, -s, k)
                self.recv(r, self.p1s.at[ab, k, j], self.p1r.at[ab, k, j])
                self.send(r, r, self.p1s.at[ab, 4 + k, j], self.p1r.at[ab, 4 + k, j], self.ax(1, ab, s))
    def p2s1(self, j):
        l = self.stage_layer(j)
        for ab in (0, 1):
            for k, s in enumerate((1, -1)):
                self.recv(self.slh(l, ab, -s, 1 - k), self.p1s.at[ab, 2 + k, j], self.p1r.at[ab, 2 + k, j])
                self.recv(self.slh(l, ab, 2, k), self.p1s.at[ab, 4 + k, j], self.p1r.at[ab, 4 + k, j])
        for n in (0, 1):
            for k, s in enumerate((1, -1)):
                for ab in (0, 1):
                    h = k if n == 0 else 1 - k
                    r = self.blkh(l, ab, 0, h)
                    self.send(r, r, self.p2s.at[ab, 2 * n + k, j], self.p2r.at[ab, 2 * n + k, j], self.ax(2, ab, s))
        for ab in (0, 1):
            self.dd_send(self.blk(l, ab, 0), ab * 4, j)
    def p2s2(self, j):
        l = self.stage_layer(j)
        for k, s in enumerate((1, -1)):
            for ab in (0, 1):
                r = self.blkh(l, ab, -s, k)
                self.recv(r, self.p2s.at[ab, k, j], self.p2r.at[ab, k, j])
                self.send(r, r, self.p2s.at[ab, 4 + k, j], self.p2r.at[ab, 4 + k, j], self.ax(2, ab, s))
    def fin(self, j):
        l = self.stage_layer(j)
        for ab in (0, 1):
            for k, s in enumerate((1, -1)):
                self.recv(self.blkh(l, ab, -s, 1 - k), self.p2s.at[ab, 2 + k, j], self.p2r.at[ab, 2 + k, j])
                self.dd_send(self.blk(l, ab, -s), ab * 4 + 1 + k, j)
        for ab in (0, 1):
            for k in (0, 1):
                self.recv(self.blkh(l, ab, 2, k), self.p2s.at[ab, 4 + k, j], self.p2r.at[ab, 4 + k, j])
            self.dd_send(self.blk(l, ab, 2), ab * 4 + 3, j)
    def other(self):
        g = Gather.__new__(Gather)
        g.__dict__.update(self.__dict__)
        g.c = 1 - self.c
        return g
    def qkv_ready(self, j):
        g = self.other()
        l = self.stage_layer(j)
        for ab in (0, 1):
            for n, k in ((0, 0), (1, -1), (2, 1), (3, 2)):
                self.recv(g.blk(l, ab, k), self.ds.at[ab * 4 + n, j], self.dr.at[ab * 4 + n, j])

    def drain(self):
        def wait(items):
            for shape, ss in items:
                r = self.wq.at[0, pl.ds(0, shape[0]), pl.ds(0, shape[1])]
                self.copy(r, r, ss, self.dr.at[0, 0], self.dev(dc=1)).wait_send()

        for key in dict.fromkeys(k for k, _, _ in self.pending):
            items = [(shape, ss) for k, shape, ss in self.pending if k == key]
            if key == "all":
                wait(items)
            else:
                met = functools.reduce(jnp.logical_and, [self.conds[k] for k in key.split()])
                pl.when(met)(functools.partial(wait, items))


def norm_into(x_ref, gain, h_ref, m):
    @pl.loop(0, m // 256)
    def _(i):
        r = pl.ds(pl.multiple_of(i * 256, 256), 256)
        v = x_ref[r, :].astype(F32)
        ms = jnp.mean(v * v, axis=-1, keepdims=True)
        h_ref[r, :] = (v * lax.rsqrt(ms + 1e-06) * gain).astype(BF)

def qkv_into(h_ref, w_ref, qkv_ref, m, tn=3072):
    @pl.loop(0, 3072 // tn)
    def _(i):
        cidx = pl.ds(pl.multiple_of(i * tn, tn), tn)
        qkv_ref[pl.ds(0, m), cidx] = jnp.dot(h_ref[pl.ds(0, m), :], w_ref[:, cidx], preferred_element_type=F32).astype(BF)

def out_into(ctx_ref, w_ref, x_ref, y_ref, m, tn=1024):
    @pl.loop(0, 1024 // tn)
    def _(i):
        cidx = pl.ds(pl.multiple_of(i * tn, tn), tn)
        u = jnp.dot(ctx_ref[pl.ds(0, m), :], w_ref[:, cidx], preferred_element_type=F32)
        y_ref[pl.ds(0, m), cidx] = (x_ref[pl.ds(0, m), cidx].astype(F32) + u).astype(BF)

def attend(q2, k2, v2, mask, lo, ind):
    z = jnp.zeros((), BF)
    kk = jnp.concatenate([jnp.where(lo, k2, z), jnp.where(lo, z, k2)], axis=0)
    vv = jnp.concatenate([jnp.where(lo, v2, z), jnp.where(lo, z, v2)], axis=0)
    vv = jnp.concatenate([vv, ind], axis=1)
    s = lax.dot_general(q2, kk, (((1,), (1,)), ((), ())), preferred_element_type=F32)
    if mask is not None:
        s = jnp.where(mask, s, -1e30)
    halves = []
    for n in (0, 1):
        t = s[:, n * 128:n * 128 + 128]
        t = jnp.exp2((t - jnp.max(t, axis=-1, keepdims=True)) * 0.18033688011112042)
        halves.append(t.astype(BF))
    o = jnp.dot(jnp.concatenate(halves, axis=1), vv, preferred_element_type=F32)
    return (o[:, :128] / o[:, 128:]).astype(BF)

def attention_into(kind, qkv_ref, ctx_ref, blocks, pairs=1):
    lo = lax.broadcasted_iota(jnp.int32, (128, 128), 1) < 64
    one, z = jnp.ones((), BF), jnp.zeros((), BF)
    ind = jnp.concatenate([jnp.where(lo, one, z), jnp.where(lo, z, one)], axis=0)
    i = lax.broadcasted_iota(jnp.int32, (128, 256), 0)
    j = lax.rem(lax.broadcasted_iota(jnp.int32, (128, 256), 1), 128)
    mask = None
    if kind == "frame":
        mask = lax.rem(i, 32) == lax.rem(j, 32)
    if kind == "row":
        mask = (lax.rem(i, 8) == lax.rem(j, 8)) & (i >= j)
    @pl.loop(0, HEADS // 2 // pairs)
    def _(step):
        for p in range(pairs):
            for b in range(blocks):
                first = (step * pairs + p) * 128

                def get(base):
                    c = pl.ds(pl.multiple_of(base + first, 128), 128)
                    if kind == "frame":
                        parts = [qkv_ref[pl.ds(f * 128 + b * 32, 32), c] for f in range(4)]
                        return jnp.concatenate(parts, axis=0)
                    return qkv_ref[pl.ds(b * 128, 128), c]

                o = attend(get(0), get(1024), get(2048), mask, lo, ind)
                c = pl.ds(pl.multiple_of(first, 128), 128)
                if kind == "frame":
                    for f in range(4):
                        ctx_ref[pl.ds(f * 128 + b * 32, 32), c] = o[f * 32 : f * 32 + 32]
                else:
                    ctx_ref[pl.ds(b * 128, 128), c] = o


def select_matrix(owner_row, owner_col, pick_ref):
    before = lax.broadcasted_iota(jnp.int32, (128, 128), 0) < lax.broadcasted_iota(jnp.int32, (128, 128), 1)
    alike = (owner_col == owner_row) & before
    slot = jnp.sum(jnp.where(alike, 1.0, 0.0), axis=0, keepdims=True)
    code = owner_row.astype(F32) * 8.0 + slot
    code = jnp.concatenate([code, code], axis=1)
    k = lax.broadcasted_iota(jnp.int32, (512, 256), 0)
    r = lax.broadcasted_iota(jnp.int32, (512, 256), 1)
    want = ((k // 16) * 8 + lax.rem(k, 8)).astype(F32)
    hit = (code == want) & (lax.rem(k // 8, 2) == r // 128)
    pick_ref[...] = jnp.where(hit, 1.0, 0.0).astype(BF)


def kernel(
    order, frames_in, owner_row, owner_col, wq_in, wo_in, g_in, out,
    wq, wo, g_all, frames, x1, pick, send, vol, h, qkv, *sems
):
    g = Gather(wq_in, wo_in, wq, wo, sems)

    def columns_first(t):
        x1[t] = frames[order[3 - t]].reshape(256, 1024)
        norm_into(x1.at[t], g_all[0], h, 256)
        qkv_into(h, wq.at[0], qkv, 256)

    def columns_rest(t):
        attention_into("column", qkv, h, 2, 4)
        out_into(h, wo.at[0], x1.at[t], x1.at[t], 256)

    def exchange_start():
        @pl.loop(0, 2)
        def _(i):
            c = pl.ds(pl.multiple_of(i * 512, 512), 512)
            send[:, c] = jnp.dot(pick[...], x1[g.x, :, c], preferred_element_type=F32).astype(BF)

        g.exchange_start(send, vol)

    def at0(*steps):
        @g.when("x0")
        def _():
            for step in steps:
                step()

    part = functools.partial
    g.greet()
    own = g.own_copies(frames_in, frames, g_in, g_all)
    for cp in own:
        cp.start()
    select_matrix(owner_row[...], owner_col[...], pick)
    g.greeted()
    g.start_x()
    gains = g.gains_copies(g_in, g_all)
    for cp in gains:
        cp.start()
    at0(*(cp.wait for cp in own))

    def send_columns(t):
        columns_rest(t)
        g.columns_send(x1, t)

    at0(
        part(columns_first, 2),
        g.x_forward_qkv,
        part(g.slices_ready, 0),
        part(g.p1s1, 0),
        part(send_columns, 2),
        part(g.slices_ready, 1),
        part(g.p1s1, 1),
        part(g.p1s2, 0),
        part(columns_first, 3),
        part(g.slices_ready, 2),
        part(g.p1s1, 2),
        part(g.p1s2, 1),
        part(send_columns, 3),
        part(g.p2s1, 0),
        part(columns_first, 1),
        part(g.p1s2, 2),
        part(send_columns, 1),
        part(g.p2s1, 1),
        part(columns_first, 0),
        part(g.p2s2, 0),
        part(columns_rest, 0),
        exchange_start,
        g.wo_forward,
        part(g.fin, 0),
        part(g.p2s2, 1),
        part(g.p2s1, 2),
    )

    @g.when("own")
    def _():
        g.x_forward_qkv()
        g.slices_ready(0)
        g.p1s1(0)
        g.slices_ready(1)
        g.p1s1(1)
        g.wo_own(0)
        g.p1s2(0)
        g.p1s2(1)
        g.p2s1(0)
        g.columns_relay(x1)
        g.p2s2(0)
        g.wo_forward()
        g.wo_own(1)
        g.columns_wait(x1)
        exchange_start()
        g.p2s1(1)
        g.fin(0)

    def own_do(step, j):
        g.when("own")(part(step, j))

    @g.when("own")
    def _():
        for cp in own:
            cp.wait()

    g.gains_wait(g_all)
    g.exchange_wait(send, vol)
    norm_into(vol, g_all[1], h, 512)
    g.qkv_ready(0)
    qkv_into(h, wq.at[1], qkv, 512)
    own_do(g.p2s2, 1)
    at0(part(g.fin, 1))
    attention_into("frame", qkv, h, 4, 8)
    at0(part(g.p2s2, 2))
    g.wo_ready(1)
    out_into(h, wo.at[1], vol, vol, 512)
    own_do(g.fin, 1)
    norm_into(vol, g_all[2], h, 512)
    g.qkv_ready(1)
    qkv_into(h, wq.at[2], qkv, 512)
    attention_into("row", qkv, h, 4, 8)
    g.wo_ready(2)
    out_into(h, wo.at[2], vol, vol, 512)
    at0(part(g.fin, 2))
    norm_into(vol, g_all[3], h, 512)
    at0(part(g.qkv_ready, 2))
    g.wo_ready(3)
    qkv_into(h, wq.at[3], qkv, 512)
    attention_into("row", qkv, h, 4, 8)
    out_into(h, wo.at[3], vol, out, 512)
    for cp in gains:
        cp.wait_send()
    g.exchange_drain(send, vol)
    g.drain()


def local(frames_in, order, owner, qkv_weight, out_weight, gains):
    vmem = pl.BlockSpec(memory_space=pltpu.VMEM)
    hbm = pl.BlockSpec(memory_space=pl.ANY)
    dma = pltpu.SemaphoreType.DMA
    result = pl.pallas_call(
        kernel,
        out_shape=jax.ShapeDtypeStruct((512, 1024), BF),
        in_specs=[pl.BlockSpec(memory_space=pltpu.SMEM), hbm, vmem, vmem, hbm, hbm, hbm],
        out_specs=vmem,
        scratch_shapes=[
            pltpu.VMEM((4, 1024, 3072), BF),
            pltpu.VMEM((4, 1024, 1024), BF),
            pltpu.VMEM((4, 1, 1024), F32),
            pltpu.VMEM((4, 2, 128, 1024), BF),
            pltpu.VMEM((4, 256, 1024), BF),
            pltpu.VMEM((512, 256), BF),
            pltpu.VMEM((512, 1024), BF),
            pltpu.VMEM((512, 1024), BF),
            pltpu.VMEM((512, 1024), BF),
            pltpu.VMEM((512, 3072), BF),
            dma((4, 3)), dma((4, 3)),
            dma((2, 6, 3)), dma((2, 6, 3)),
            dma((2, 6, 3)), dma((2, 6, 3)),
            dma((10, 3)), dma((10, 3)),
            dma((6,)), dma((6,)),
            dma((3,)), dma((3,)),
            dma((32,)), dma((32,)),
            dma((4,)),
        ],
        compiler_params=pltpu.CompilerParams(
            collective_id=0, has_side_effects=True, vmem_limit_bytes=60 * 1024 * 1024
        ),
    )(order, frames_in, owner[None, :], owner[:, None], qkv_weight, out_weight, gains)
    return result.reshape(1, 64, 8, 1024)


def solution(mesh):
    placed = (
        P(None, "seq", None, None),
        P(),
        P(),
        P("section", None, None),
        P("section", None, None),
        P("section", None),
    )
    return jax.shard_map(
        local,
        mesh=mesh,
        in_specs=placed,
        out_specs=P("section", None, "seq", None),
        check_vma=False,
    )
```
